256 devices in a mesh: ctx: 64 (over x, z, core), head: 4 (over y).
Axes of the slice: x: 4, y: 4, z: 8, core: 2. Of those that a mesh axis runs over, the one named last changes fastest.
Arguments:
- mixer_input: bfloat16 [32768, 4096], P('ctx', 'head'), may hold values from -61 to 61
- gate_input: bfloat16 [32768, 4096], P('ctx', 'head'), may hold values from -7.5 to 7.5
- write_vecs: bfloat16 [32768, 128], P('ctx'), may hold values from -0.8984375 to 0.8984375
- read_vecs: bfloat16 [32768, 128], P('ctx'), may hold values from -0.8984375 to 0.8984375
- log_decay: float32 [64, 32768], P('head', 'ctx'), may hold values from -0.76 to 0
- doc_start: int32 [32768], P('ctx'), may hold values from 0 to 1, as said below
- live_mask: int32 [32768], P('ctx'), may hold values from 0 to 1, as said below
- skip_gain: float32 [64], P('head'), may hold values from 0.5 to 2
- norm_gain: float32 [4096], P('head'), may hold values from 0.25 to 1.75
- residual: bfloat16 [32768, 2048], P('ctx', 'head'), may hold values from -61 to 61
- out_weight: bfloat16 [4096, 2048], P(('head', 'ctx')), may hold values from -0.09375 to 0.09375
- mlp_gain: float32 [2048], replicated, may hold values from 0.25 to 1.75
- gate_weight: bfloat16 [2048, 4096], P('ctx', 'head'), may hold values from -0.125 to 0.125
- up_weight: bfloat16 [2048, 4096], P('ctx', 'head'), may hold values from -0.125 to 0.125
- down_weight: bfloat16 [4096, 2048], P(('head', 'ctx')), may hold values from -0.09375 to 0.09375
Outputs:
- mixed: bfloat16 [32768, 2048], P('ctx', 'head')
The draws below stay inside these ranges and needn't reach their ends.
Inputs may be any that keep to these rules, and one draw needn't show every extreme that they name: `doc_start`: documents begin only at the first token of a group of 256; the window's first token begins one; a document spans at most 16 groups, and some document spans exactly that many. `live_mask`: the 0 entries are the tokens after a document's last real token, all within its last group; every document has a real token.
All inputs are finite; a program needn't handle non-finite values.
Results may differ from the reference program's by a relative error of at most 0.007.
Values may be sent and summed in bfloat16 or wider, within the bound.
No kernel may reach another device: no remote copies, remote signals or barrier semaphores. Data moves between devices by JAX's collectives and lax.ppermute only.
A program may use at most 128 MiB of HBM per device.

```python
import math
import jax
import jax.numpy as jnp
from jax import lax

D = 2048
SSM_CHANNEL_NUM = 64
HDIM = 64
STATE = 128
FF = 4096
GROUP = 256
DOC_GROUPS = 16
TOK_DEV = 512
CONTEXT_POSITION = 32768
INNER = 4096
N_CTX = 64


def doc_layout(key):
    group_count = CONTEXT_POSITION // GROUP
    key_lengths = jax.random.fold_in(key, 101)
    key_pick = jax.random.fold_in(key, 102)
    key_padding = jax.random.fold_in(key, 103)
    lengths = jax.random.randint(key_lengths, (group_count,), 1, DOC_GROUPS + 1)
    longest = jax.random.randint(key_pick, (), 0, max(1, group_count // DOC_GROUPS - 1))
    lengths = jnp.where(jnp.arange(group_count) == longest, DOC_GROUPS, lengths).astype(jnp.int32)
    ends = jnp.cumsum(lengths).astype(jnp.int32)
    begins = ends - lengths
    first_group = jnp.zeros((group_count,), jnp.int32).at[begins].set(1, mode='drop')
    closing = jnp.concatenate([first_group[1:], jnp.ones((1,), jnp.int32)])
    padding = jax.random.randint(key_padding, (group_count,), 0, GROUP)
    offsets = jnp.arange(GROUP, dtype=jnp.int32)
    starts = first_group[:, None] * (offsets[None, :] == 0).astype(jnp.int32)
    real_tokens = jnp.where(closing[:, None] == 1, (offsets[None, :] < GROUP - padding[:, None]).astype(jnp.int32), 1)
    return (starts.reshape(-1).astype(jnp.int32), real_tokens.reshape(-1).astype(jnp.int32))


def scaled_field(key, row_count, col_count):
    key_rows = jax.random.fold_in(key, 201)
    key_cols = jax.random.fold_in(key, 202)
    key_noise = jax.random.fold_in(key, 203)
    row_scale = jnp.exp(jax.random.uniform(key_rows, (row_count, 1), jnp.float32, math.log(0.3), math.log(3.0)))
    ramp = 0.6 * jnp.power(3.0, jnp.arange(col_count, dtype=jnp.float32) / col_count)
    col_scale = ramp[None, :] * jnp.exp(jax.random.uniform(key_cols, (1, col_count), jnp.float32, math.log(0.5), math.log(2.0)))
    noise = jnp.clip(jax.random.normal(key_noise, (row_count, col_count), jnp.float32), -4.0, 4.0)
    return noise * row_scale * col_scale


def draw_mixer_input(key, part):
    return scaled_field(key, CONTEXT_POSITION, INNER).astype(jnp.bfloat16)


def draw_residual(key, part):
    return scaled_field(key, CONTEXT_POSITION, D).astype(jnp.bfloat16)


def draw_doc_start(key, part):
    return doc_layout(key)[0]


def draw_live_mask(key, part):
    return doc_layout(key)[1]


def draw_log_decay(key, part):
    sequence_span = DOC_GROUPS * GROUP
    fast_share = 0.5
    key_kind = jax.random.fold_in(key, 301)
    key_fast = jax.random.fold_in(key, 302)
    key_slow = jax.random.fold_in(key, 303)
    key_jitter = jax.random.fold_in(key, 304)
    spike_seed = jax.random.fold_in(key, 305)
    key_depth = jax.random.fold_in(key, 306)
    is_fast = jax.random.uniform(key_kind, (SSM_CHANNEL_NUM, 1), jnp.float32) < fast_share
    fast_rate = jnp.exp(jax.random.uniform(key_fast, (SSM_CHANNEL_NUM, 1), jnp.float32, math.log(1.0 / 50.0), math.log(1.0 / 30.0)))
    slow_rate = jnp.exp(jax.random.uniform(key_slow, (SSM_CHANNEL_NUM, 1), jnp.float32, math.log(0.1), 0.0)) / sequence_span
    ground_frequency = jnp.where(is_fast, fast_rate, slow_rate)
    jitter_perturbation = jnp.exp(jax.random.uniform(key_jitter, (SSM_CHANNEL_NUM, CONTEXT_POSITION), jnp.float32, math.log(0.5), math.log(2.0)))
    spike_occurrences = (jax.random.uniform(spike_seed, (SSM_CHANNEL_NUM, CONTEXT_POSITION), jnp.float32) < 3.0 / sequence_span).astype(jnp.float32)
    level_ordinal = jax.random.uniform(key_depth, (SSM_CHANNEL_NUM, CONTEXT_POSITION), jnp.float32, 0.22, 0.69)
    return -(ground_frequency * jitter_perturbation + spike_occurrences * level_ordinal)


def shard_levels(own_key, dims, split, low, top_value):
    loudness = 1.0
    for dim, shards_of in split:
        steps = jax.random.uniform(jax.random.fold_in(jax.random.fold_in(own_key, 6), dim), (shards_of,), jnp.float32, low / len(split), top_value / len(split))
        loudness = loudness * jnp.repeat(jnp.exp(steps), dims[dim] // shards_of).reshape((-1,) + (1,) * (len(dims) - 1 - dim))
    return loudness


def centred(own_key, shape, spread, reach, cuts=(), kind=jnp.bfloat16):
    level = shard_levels(own_key, shape, cuts, -0.22, 0.18) if cuts else 1.0
    array = jax.random.normal(own_key, shape, jnp.float32) * spread * level
    return jnp.minimum(jnp.maximum(array, -reach), reach).astype(kind)


def setup_inputs(seed: int = 0) -> dict:
    key_list = jax.random.split(jax.random.key(seed), 16)
    return {
        "mixer_input": draw_mixer_input(jax.random.fold_in(key_list[15], 71), 0),
        "gate_input": centred(key_list[1], (CONTEXT_POSITION, INNER), 1.5, 7.5, ((0, 64), (1, 4))),
        "write_vecs": centred(key_list[2], (CONTEXT_POSITION, STATE), 0.15, 0.8984375, ((0, 64),)),
        "read_vecs": centred(key_list[3], (CONTEXT_POSITION, STATE), 0.15, 0.8984375, ((0, 64),)),
        "log_decay": draw_log_decay(jax.random.fold_in(key_list[15], 71), 0),
        "doc_start": draw_doc_start(jax.random.fold_in(key_list[15], 71), 0),
        "live_mask": draw_live_mask(jax.random.fold_in(key_list[15], 71), 0),
        "skip_gain": jnp.clip(jnp.exp(math.log(2.0) - 1.3862944 * jax.random.uniform(key_list[7], (SSM_CHANNEL_NUM,), jnp.float32) ** shard_levels(key_list[7], (SSM_CHANNEL_NUM,), ((0, 4),), -0.2, 0.2)), 0.5, 2.0),
        "norm_gain": jnp.clip(1.0 + 0.15 * jax.random.normal(key_list[8], (INNER,), jnp.float32), 0.25, 1.75),
        "residual": draw_residual(jax.random.fold_in(key_list[15], 71), 0),
        "out_weight": centred(key_list[10], (INNER, D), INNER ** -0.5, 0.09375, ((0, 256),)),
        "mlp_gain": jnp.clip(1.0 + 0.15 * jax.random.normal(key_list[11], (D,), jnp.float32), 0.25, 1.75),
        "gate_weight": centred(key_list[12], (D, FF), D ** -0.5, 0.125, ((0, 64), (1, 4))),
        "up_weight": centred(key_list[13], (D, FF), D ** -0.5, 0.125, ((0, 64), (1, 4))),
        "down_weight": centred(key_list[14], (FF, D), FF ** -0.5, 0.09375, ((0, 256),)),
    }


EPS = 1e-05

def group_core(masked, write_group, read_group, log_group, start_group, skip_gain):
    positions = jnp.arange(GROUP)
    log_sums = jnp.cumsum(log_group, axis=1)
    doc_index = jnp.cumsum(start_group)
    same_doc = (doc_index[:, None] == doc_index[None, :]) & (positions[:, None] >= positions[None, :])
    scores = jnp.dot(read_group, write_group.T, preferred_element_type=jnp.float32)
    log_gaps = jnp.where(same_doc[None], log_sums[:, :, None] - log_sums[:, None, :], 0.0)
    weights = jnp.where(same_doc[None], scores[None] * jnp.exp(log_gaps), 0.0).astype(jnp.bfloat16)
    per_head = masked.reshape(GROUP, -1, HDIM)
    intra_out = jnp.einsum('hij,jhp->ihp', weights.astype(jnp.float32), per_head.astype(jnp.float32))
    tail_wts = jnp.exp(log_sums[:, -1:] - log_sums) * (doc_index == doc_index[-1]).astype(jnp.float32)[None]
    weighted = (write_group.astype(jnp.float32)[None] * tail_wts[:, :, None]).astype(jnp.bfloat16)
    local_state = jnp.einsum('hjn,jhp->hnp', weighted.astype(jnp.float32), per_head.astype(jnp.float32))
    reach_wts = jnp.exp(log_sums) * (doc_index == 0).astype(jnp.float32)[None]
    decay_all = jnp.exp(log_sums[:, -1]) * (doc_index[-1] == 0).astype(jnp.float32)
    direct = intra_out + skip_gain[None, :, None] * per_head.astype(jnp.float32)
    return (direct, local_state, reach_wts, decay_all)

def reference(mixer_input, gate_input, write_vecs, read_vecs, log_decay, doc_start, live_mask, skip_gain, norm_gain, residual, out_weight, mlp_gain, gate_weight, up_weight, down_weight):
    group_count = CONTEXT_POSITION // GROUP
    masked = mixer_input * live_mask.astype(jnp.bfloat16)[:, None]
    group_data = (masked.reshape(group_count, GROUP, INNER), gate_input.reshape(group_count, GROUP, INNER), write_vecs.reshape(group_count, GROUP, STATE), read_vecs.reshape(group_count, GROUP, STATE), log_decay.reshape(SSM_CHANNEL_NUM, group_count, GROUP).transpose(1, 0, 2), doc_start.reshape(group_count, GROUP))

    def advance(carried, pieces):
        x_group, z_group, write_group, read_group, log_group, start_group = pieces
        direct, local_state, reach_wts, decay_all = group_core(x_group, write_group, read_group, log_group, start_group, skip_gain)
        inner_state = carried.astype(jnp.bfloat16)
        crossed = jnp.einsum('in,hnp->ihp', read_group.astype(jnp.float32), inner_state.astype(jnp.float32)) * reach_wts.T[:, :, None]
        output = (direct + crossed).reshape(GROUP, INNER)
        gated = output * jax.nn.silu(z_group.astype(jnp.float32))
        normed = (gated * lax.rsqrt(lax.optimization_barrier(jnp.mean(gated * gated, axis=1, keepdims=True)) + EPS) * norm_gain).astype(jnp.bfloat16)
        return (decay_all[:, None, None] * carried + local_state, normed)
    initial = jnp.zeros((SSM_CHANNEL_NUM, STATE, HDIM), jnp.float32)
    unused, normed = lax.scan(advance, initial, group_data)

    def mlp_block(block_data):
        normed_rows, resid_rows, live_rows = block_data
        hidden = (resid_rows.astype(jnp.float32) + jnp.dot(normed_rows, out_weight, preferred_element_type=jnp.float32)).astype(jnp.bfloat16)
        hidden_f = hidden.astype(jnp.float32)
        scaled = (hidden_f * lax.rsqrt(lax.optimization_barrier(jnp.mean(hidden_f * hidden_f, axis=1, keepdims=True)) + EPS) * mlp_gain).astype(jnp.bfloat16)
        gate_out = jnp.dot(scaled, gate_weight, preferred_element_type=jnp.float32)
        up_out = jnp.dot(scaled, up_weight, preferred_element_type=jnp.float32)
        act = (jax.nn.silu(gate_out) * up_out).astype(jnp.bfloat16)
        down_out = jnp.dot(act, down_weight, preferred_element_type=jnp.float32)
        return (live_rows.astype(jnp.float32)[:, None] * (hidden_f + down_out)).astype(jnp.bfloat16)
    blocks = (normed.reshape(N_CTX, TOK_DEV, INNER), residual.reshape(N_CTX, TOK_DEV, D), live_mask.reshape(N_CTX, TOK_DEV))
    mixed = lax.map(mlp_block, blocks)
    return mixed.reshape(CONTEXT_POSITION, D)
```

```python
import jax
import jax.numpy as jnp
from jax import lax
from jax.experimental import pallas as pl
from jax.experimental.pallas import tpu as pltpu
from jax.sharding import PartitionSpec as P

HDIM = 64
STATE = 128
GROUP = 256
DOC_GROUPS = 16
INNER = 4096
EPS = 1e-05
F32 = jnp.float32
BF16 = jnp.bfloat16


def params(mib=48):
    return pltpu.CompilerParams(vmem_limit_bytes=mib * 1024 * 1024)


def vmem():
    return pl.BlockSpec(memory_space=pltpu.VMEM)


def contract(a, b, da, db):
    return lax.dot_general(a, b, (((da,), (db,)), ((), ())), preferred_element_type=F32)


def split2(v):
    hi = v.astype(BF16)
    return hi, (v - hi.astype(F32)).astype(BF16)


def split3(v):
    hi = v.astype(BF16)
    rest = v - hi.astype(F32)
    mid = rest.astype(BF16)
    return hi, mid, (rest - mid.astype(F32)).astype(BF16)


def tri_ones(n):
    rows = lax.broadcasted_iota(jnp.int32, (n, n), 0)
    cols = lax.broadcasted_iota(jnp.int32, (n, n), 1)
    return jnp.where(rows >= cols, 1.0, 0.0).astype(BF16), jnp.where(rows == cols, 1.0, 0.0).astype(BF16)


def head_spread(heads):
    rows = lax.broadcasted_iota(jnp.int32, (heads, heads * HDIM), 0)
    cols = lax.broadcasted_iota(jnp.int32, (heads, heads * HDIM), 1)
    return jnp.where(cols // HDIM == rows, 1.0, 0.0).astype(BF16)


def spread_wide(cols, spread):
    hi, lo = split2(cols)
    return contract(hi, spread, 1, 0) + contract(lo, spread, 1, 0)


def sums_by_row(log_group, tri):
    return sum(contract(part, tri, 1, 1) for part in split3(log_group))


def sums_by_column(log_group, tri):
    return sum(contract(tri, part, 1, 1) for part in split3(log_group))


def column_of(row, eye):
    return contract(eye, jnp.broadcast_to(row, (16, row.shape[1])).astype(BF16), 1, 1)


def state_kernel(x_ref, write_ref, log_ref, start_ref, live_ref, pay_ref, local_ref, dec_ref):
    heads = log_ref.shape[0]
    tri, eye = tri_ones(GROUP)
    spread = head_spread(heads)
    locals_, decays = [], []
    for g in range(2):
        rows = slice(g * GROUP, (g + 1) * GROUP)
        sums = sums_by_column(log_ref[:, rows], tri)
        last = sums[GROUP - 1 : GROUP, :]
        live = column_of(live_ref[:, rows], eye)
        tail = spread_wide(jnp.exp(last - sums) * live, spread)
        scaled = (x_ref[rows, :].astype(F32) * tail).astype(BF16)
        locals_.append(contract(write_ref[rows, :], scaled, 0, 0))
        fresh = 1.0 - start_ref[:, g * GROUP : g * GROUP + 1]
        end = jnp.broadcast_to(jnp.exp(last) * fresh, (16, heads))
        decays.append(sum(contract(part, spread, 1, 0) for part in split3(end)))
    state = decays[1][0:1] * locals_[0] + locals_[1]
    pay_ref[0:STATE, :] = state.astype(BF16)
    both = decays[0] * decays[1]
    hi, mid, low = split3(both)
    row = lax.broadcasted_iota(jnp.int32, both.shape, 0)
    packed = jnp.where(row == 0, hi.astype(F32), jnp.where(row == 1, mid.astype(F32), low.astype(F32)))
    pay_ref[STATE : STATE + 16, :] = packed.astype(BF16)
    local_ref[...] = locals_[0]
    dec_ref[...] = decays[0][0:8]


def join_kernel(own_ref, got_ref, out_ref):
    def factor(ref):
        tail = ref[STATE : STATE + 16, :].astype(F32)
        return tail[0:1] + tail[1:2] + tail[2:3]

    mine = factor(own_ref)
    state = own_ref[0:STATE, :].astype(F32) + mine * got_ref[0:STATE, :].astype(F32)
    out_ref[0:STATE, :] = state.astype(BF16)
    both = jnp.broadcast_to(mine * factor(got_ref), (16, own_ref.shape[1]))
    hi, mid, low = split3(both)
    row = lax.broadcasted_iota(jnp.int32, both.shape, 0)
    packed = jnp.where(row == 0, hi.astype(F32), jnp.where(row == 1, mid.astype(F32), low.astype(F32)))
    out_ref[STATE : STATE + 16, :] = packed.astype(BF16)


def intra_kernel(x_ref, write_ref, read_ref, log_ref, live_ref, skip_ref, out_ref):
    heads = log_ref.shape[0]
    tri, eye = tri_ones(GROUP)
    half = GROUP // 2
    live = column_of(live_ref[...], eye)[:, 0:1].astype(BF16)
    by_row = sums_by_row(log_ref[...], tri)
    by_col = sums_by_column(log_ref[...], tri)
    scores = contract(read_ref[...], write_ref[...], 1, 1)
    scores = jnp.where(tri > 0, scores, 0.0)
    lane = lax.broadcasted_iota(jnp.int32, (GROUP, 2 * HDIM), 1)
    for pair in range(heads // 2):
        cols = slice(pair * 2 * HDIM, (pair + 1) * 2 * HDIM)
        x = x_ref[:, cols] * live
        top = bottom = 0.0
        for k in range(2):
            h = 2 * pair + k
            mine = jnp.where((lane < HDIM) == (k == 0), x, jnp.zeros_like(x))
            row = by_row[h : h + 1, :]
            col = by_col[:, h : h + 1]
            gap = jnp.minimum(col[:half] - row[:, :half], 0.0)
            w = (scores[:half, :half] * jnp.exp(gap)).astype(BF16)
            top = top + contract(w, mine[:half], 1, 0)
            gap = jnp.minimum(col[half:] - row, 0.0)
            w = (scores[half:] * jnp.exp(gap)).astype(BF16)
            bottom = bottom + contract(w, mine, 1, 0)
        direct = skip_ref[:, cols] * x.astype(F32)
        out_ref[:half, cols] = top + direct[:half]
        out_ref[half:, cols] = bottom + direct[half:]


def gate_kernel(direct_ref, got_ref, local_ref, dec_ref, read_ref, log_ref, start_ref, gate_ref, gain_ref, out_ref, sq_ref):
    heads = log_ref.shape[0]
    tri, _ = tri_ones(GROUP)
    spread = head_spread(heads)
    second = (pl.program_id(0) > 0).astype(F32)
    arriving = got_ref[0:STATE, :].astype(F32)
    carried = (1.0 - second + second * dec_ref[0:1, :]) * arriving + second * local_ref[...]
    crossed = contract(read_ref[...], carried.astype(BF16), 1, 0)
    fresh = 1.0 - start_ref[:, 0:1]
    reach = spread_wide(jnp.exp(sums_by_column(log_ref[...], tri)) * fresh, spread)
    gate = gate_ref[...].astype(F32)
    g = (direct_ref[...] + crossed * reach) * (gate / (1.0 + jnp.exp(-gate)))
    out_ref[...] = (g * gain_ref[...]).astype(BF16)
    squares = jnp.broadcast_to(jnp.sum(g * g, axis=1, keepdims=True), (GROUP, 128))
    sq_ref[...] = jnp.transpose(squares)[0:8, :]


def project_kernel(head_ref, g_ref, w_ref, out_ref):
    weights = w_ref[...].reshape(g_ref.shape[1], w_ref.shape[2])
    out_ref[...] = contract(g_ref[...], weights, 1, 0)[None]


def mlp_kernel(head_ref, own_ref, prev_ref, next_ref, far_ref, gain_ref, gate_ref, up_ref, down_ref, out_ref, x_ref, acc_ref):
    step = pl.program_id(0)
    width = own_ref.shape[1]
    head = head_ref[0]

    @pl.when(step == 0)
    def _():
        pieces = [(0, own_ref), (3, prev_ref), (1, next_ref), (2, far_ref)]
        total = 0.0
        for _, ref in pieces:
            v = ref[...].astype(F32)
            total = total + jnp.sum(v * v, axis=1, keepdims=True)
        scale = lax.rsqrt(total / (4 * width) + EPS)
        for by, ref in pieces:
            at = pl.multiple_of(((head + by) % 4) * width, width)
            x_ref[:, pl.ds(at, width)] = (ref[...].astype(F32) * scale * gain_ref[:, pl.ds(at, width)]).astype(BF16)

    x = x_ref[...]
    block = gate_ref.shape[2]
    gate = contract(x, gate_ref[...].reshape(x.shape[1], block), 1, 0)
    up = contract(x, up_ref[...].reshape(x.shape[1], block), 1, 0)
    act = (gate / (1.0 + jnp.exp(-gate)) * up).astype(BF16)
    part = contract(act, down_ref[...].reshape(block, x.shape[1]), 1, 0)

    @pl.when(step == 0)
    def _():
        acc_ref[...] = part

    @pl.when(step > 0)
    def _():
        acc_ref[...] += part

    @pl.when(step == pl.num_programs(0) - 1)
    def _():
        for k in range(4):
            at = pl.multiple_of(((head + k) % 4) * width, width)
            out_ref[k] = acc_ref[:, pl.ds(at, width)].astype(BF16)


def sent(array, by):
    return lax.ppermute(array, "head", [(i, (i + by) % 4) for i in range(4)])


def scattered(parts):
    half = parts[0].shape[0] // 2
    first = sent(parts[2][:half].astype(BF16), 1)
    second = sent(parts[2][half:].astype(BF16), -1)
    one = jnp.concatenate([parts[1][:half].astype(F32) + first.astype(F32), parts[1][half:].astype(F32)], 0).astype(BF16)
    three = jnp.concatenate([parts[3][:half].astype(F32), parts[3][half:].astype(F32) + second.astype(F32)], 0).astype(BF16)
    return parts[0].astype(F32) + sent(one, 1).astype(F32) + sent(three, -1).astype(F32)


def gathered(mine):
    half = mine.shape[0] // 2
    prev = sent(mine, 1)
    following = sent(mine, -1)
    far = jnp.concatenate([sent(prev[:half], 1), sent(following[half:], -1)], 0)
    return prev, following, far


def shards(
    mixer_input,
    gate_input,
    write_vecs,
    read_vecs,
    log_decay,
    doc_start,
    live_mask,
    skip_gain,
    norm_gain,
    residual,
    out_weight,
    mlp_gain,
    gate_weight,
    up_weight,
    down_weight,
):
    tokens, inner = mixer_input.shape
    heads = log_decay.shape[0]
    peers = lax.axis_size("ctx")
    width = residual.shape[1]
    model = out_weight.shape[1]
    units = gate_weight.shape[1]
    in_rows, ff_rows, out_rows = gate_weight.shape[0], down_weight.shape[0], out_weight.shape[0]
    packed_rows = in_rows + ff_rows + out_rows

    packed = jnp.concatenate(
        [jnp.concatenate([gate_weight, up_weight], 1), down_weight, out_weight], 0
    )
    weights = lax.all_gather(packed, "ctx", axis=0)

    starts = doc_start.astype(F32).reshape(1, tokens)
    live = live_mask.astype(F32).reshape(1, tokens)
    skip = jnp.repeat(skip_gain, HDIM).reshape(1, inner)
    gain = norm_gain.reshape(1, inner)
    head = lax.axis_index("head").reshape(1)

    payload, local_0, dec_0 = pl.pallas_call(
        state_kernel,
        out_shape=(
            jax.ShapeDtypeStruct((STATE + 16, inner), BF16),
            jax.ShapeDtypeStruct((STATE, inner), F32),
            jax.ShapeDtypeStruct((8, inner), F32),
        ),
        in_specs=[vmem()] * 5,
        out_specs=(vmem(),) * 3,
        compiler_params=params(),
        name="state",
    )(mixer_input, write_vecs, log_decay, starts, live)

    def passed(array, by):
        return lax.ppermute(array, "ctx", [(i, i + by) for i in range(peers - by)])

    window = 1
    while window * (tokens // GROUP) < DOC_GROUPS:
        payload = pl.pallas_call(
            join_kernel,
            out_shape=jax.ShapeDtypeStruct(payload.shape, BF16),
            in_specs=[vmem()] * 2,
            out_specs=vmem(),
            compiler_params=params(),
            name="join",
        )(payload, passed(payload, window))
        window *= 2
    arriving = passed(payload[:STATE], 1)

    by_group = pl.BlockSpec((GROUP, inner), lambda g: (g, 0))
    vecs = pl.BlockSpec((GROUP, STATE), lambda g: (g, 0))
    logs = pl.BlockSpec((heads, GROUP), lambda g: (0, g))
    flags = pl.BlockSpec((1, GROUP), lambda g: (0, g))
    whole = lambda a: pl.BlockSpec(a.shape, lambda g: (0,) * a.ndim)
    direct = pl.pallas_call(
        intra_kernel,
        grid=(tokens // GROUP,),
        out_shape=jax.ShapeDtypeStruct((tokens, inner), F32),
        in_specs=[by_group, vecs, vecs, logs, flags, whole(skip)],
        out_specs=by_group,
        compiler_params=params(),
        name="intra",
    )(mixer_input, write_vecs, read_vecs, log_decay, live, skip)

    gated, squares = pl.pallas_call(
        gate_kernel,
        grid=(tokens // GROUP,),
        out_shape=(
            jax.ShapeDtypeStruct((tokens, inner), BF16),
            jax.ShapeDtypeStruct((8, tokens), F32),
        ),
        in_specs=[
            by_group,
            whole(arriving),
            whole(local_0),
            whole(dec_0),
            vecs,
            logs,
            flags,
            by_group,
            whole(gain),
        ],
        out_specs=(by_group, pl.BlockSpec((8, GROUP), lambda g: (0, g))),
        compiler_params=params(),
        name="gating",
    )(direct, arriving, local_0, dec_0, read_vecs, log_decay, starts, gate_input, gain)

    mine = squares[0]
    total = mine + sent(mine, 1) + sent(mine, -1) + sent(mine, 2)
    row_scale = lax.rsqrt(total / INNER + EPS)

    partial = pl.pallas_call(
        project_kernel,
        grid_spec=pltpu.PrefetchScalarGridSpec(
            num_scalar_prefetch=1,
            grid=(4,),
            in_specs=[
                pl.BlockSpec((tokens, inner), lambda k, h: (0, 0)),
                pl.BlockSpec(
                    (peers, out_rows, width),
                    lambda k, h: (0, (in_rows + ff_rows) // out_rows, (h[0] + (k + 2) % 4) % 4),
                ),
            ],
            out_specs=pl.BlockSpec((1, tokens, width), lambda k, h: ((k + 2) % 4, 0, 0)),
        ),
        out_shape=jax.ShapeDtypeStruct((4, tokens, width), F32),
        compiler_params=params(),
        name="project",
    )(head, gated, weights)

    ff_block = 256
    out = []
    chunk = tokens // 2
    for c in range(2):
        rows = slice(c * chunk, (c + 1) * chunk)
        summed = scattered([partial[k, rows] for k in range(4)])
        hidden = (residual[rows].astype(F32) + summed * row_scale[rows, None]).astype(BF16)
        prev, following, far = gathered(hidden)
        full = lambda a: pl.BlockSpec(a.shape, lambda j, h: (0,) * a.ndim)
        mlp_gains = mlp_gain.reshape(1, model)
        parts = pl.pallas_call(
            mlp_kernel,
            grid_spec=pltpu.PrefetchScalarGridSpec(
                num_scalar_prefetch=1,
                grid=(units // ff_block,),
                in_specs=[
                    full(hidden),
                    full(prev),
                    full(following),
                    full(far),
                    full(mlp_gains),
                    pl.BlockSpec((peers, in_rows, ff_block), lambda j, h: (0, 0, j)),
                    pl.BlockSpec((peers, in_rows, ff_block), lambda j, h: (0, 0, units // ff_block + j)),
                    pl.BlockSpec((ff_block // ff_rows, ff_rows, model), lambda j, h: (j, in_rows // ff_rows, 0)),
                ],
                out_specs=pl.BlockSpec((4, chunk, width), lambda j, h: (0, 0, 0)),
                scratch_shapes=[pltpu.VMEM((chunk, model), BF16), pltpu.VMEM((chunk, model), F32)],
            ),
            out_shape=jax.ShapeDtypeStruct((4, chunk, width), BF16),
            compiler_params=params(),
            name="mlp",
        )(head, hidden, prev, following, far, mlp_gains, weights, weights, weights)
        added = scattered([parts[k] for k in range(4)])
        out.append(
            (live_mask[rows].astype(F32)[:, None] * (hidden.astype(F32) + added)).astype(BF16)
        )
    return jnp.concatenate(out, 0)


def solution(mesh):
    return jax.shard_map(
        shards,
        mesh=mesh,
        in_specs=(
            P("ctx", "head"),
            P("ctx", "head"),
            P("ctx", None),
            P("ctx", None),
            P("head", "ctx"),
            P("ctx"),
            P("ctx"),
            P("head"),
            P("head"),
            P("ctx", "head"),
            P(("head", "ctx"), None),
            P(),
            P("ctx", "head"),
            P("ctx", "head"),
            P(("head", "ctx"), None),
        ),
        out_specs=P("ctx", "head"),
        check_vma=False,
    )
```

```python
import jax
import jax.numpy as jnp
from jax import lax
from jax.experimental import pallas as pl
from jax.experimental.pallas import tpu as pltpu
from jax.sharding import PartitionSpec as P

HDIM = 64
STATE = 128
GROUP = 256
DOC_GROUPS = 16
INNER = 4096
EPS = 1e-05
F32 = jnp.float32
BF16 = jnp.bfloat16


def params(mib=48):
    return pltpu.CompilerParams(vmem_limit_bytes=mib * 1024 * 1024)


def vmem():
    return pl.BlockSpec(memory_space=pltpu.VMEM)


def contract(a, b, da, db):
    return lax.dot_general(a, b, (((da,), (db,)), ((), ())), preferred_element_type=F32)


def split2(v):
    hi = v.astype(BF16)
    return hi, (v - hi.astype(F32)).astype(BF16)


def split3(v):
    hi = v.astype(BF16)
    rest = v - hi.astype(F32)
    mid = rest.astype(BF16)
    return hi, mid, (rest - mid.astype(F32)).astype(BF16)


def tri_ones(n):
    rows = lax.broadcasted_iota(jnp.int32, (n, n), 0)
    cols = lax.broadcasted_iota(jnp.int32, (n, n), 1)
    return jnp.where(rows >= cols, 1.0, 0.0).astype(BF16), jnp.where(rows == cols, 1.0, 0.0).astype(BF16)


def head_spread(heads):
    rows = lax.broadcasted_iota(jnp.int32, (heads, heads * HDIM), 0)
    cols = lax.broadcasted_iota(jnp.int32, (heads, heads * HDIM), 1)
    return jnp.where(cols // HDIM == rows, 1.0, 0.0).astype(BF16)


def spread_wide(cols, spread):
    hi, lo = split2(cols)
    return contract(hi, spread, 1, 0) + contract(lo, spread, 1, 0)


def sums_by_row(log_group, tri):
    return sum(contract(part, tri, 1, 1) for part in split3(log_group))


def sums_by_column(log_group, tri):
    return sum(contract(tri, part, 1, 1) for part in split3(log_group))


def column_of(row, eye):
    return contract(eye, jnp.broadcast_to(row.astype(F32), (16, row.shape[1])).astype(BF16), 1, 1)


def state_kernel(x_ref, write_ref, log_ref, start_ref, live_ref, pay_ref, local_ref, dec_ref):
    heads = log_ref.shape[0]
    tri, eye = tri_ones(GROUP)
    spread = head_spread(heads)
    locals_, decays = [], []
    for g in range(2):
        rows = slice(g * GROUP, (g + 1) * GROUP)
        sums = sums_by_column(log_ref[:, rows], tri)
        last = sums[GROUP - 1 : GROUP, :]
        live = column_of(live_ref[:, rows], eye)
        tail = spread_wide(jnp.exp(last - sums) * live, spread)
        scaled = (x_ref[rows, :].astype(F32) * tail).astype(BF16)
        locals_.append(contract(write_ref[rows, :], scaled, 0, 0))
        fresh = 1.0 - start_ref[:, g * GROUP : g * GROUP + 1].astype(F32)
        end = jnp.broadcast_to(jnp.exp(last) * fresh, (16, heads))
        decays.append(sum(contract(part, spread, 1, 0) for part in split3(end)))
    state = decays[1][0:1] * locals_[0] + locals_[1]
    pay_ref[0:STATE, :] = state.astype(BF16)
    pay_ref[STATE : STATE + 16, :] = factor_rows((decays[0] * decays[1])[0:1])
    local_ref[...] = locals_[0]
    dec_ref[...] = decays[0][0:8]


def factor_of(ref, at):
    tail = ref[at : at + 16, :].astype(F32)
    return tail[0:1] + tail[1:2] + tail[2:3]


def factor_rows(factor):
    both = jnp.broadcast_to(factor, (16, factor.shape[1]))
    hi, mid, low = split3(both)
    row = lax.broadcasted_iota(jnp.int32, both.shape, 0)
    packed = jnp.where(row == 0, hi.astype(F32), jnp.where(row == 1, mid.astype(F32), low.astype(F32)))
    return packed.astype(BF16)


def pair_kernel(where_ref, mine_ref, twin_ref, out_ref):
    core = where_ref[3]
    half = STATE // 2
    at = pl.multiple_of(core * half, half)
    mine, twin = factor_of(mine_ref, STATE), factor_of(twin_ref, STATE)
    own = mine_ref[pl.ds(at, half), :].astype(F32)
    got = twin_ref[pl.ds(at, half), :].astype(F32)
    second = (core == 1).astype(F32)
    state = second * (own + mine * got) + (1.0 - second) * (got + twin * own)
    out_ref[0:half, :] = state.astype(BF16)
    out_ref[half : half + 16, :] = factor_rows(mine * twin)


def join_kernel(own_ref, got_ref, out_ref):
    half = STATE // 2
    mine = factor_of(own_ref, half)
    state = own_ref[0:half, :].astype(F32) + mine * got_ref[0:half, :].astype(F32)
    out_ref[0:half, :] = state.astype(BF16)
    out_ref[half : half + 16, :] = factor_rows(mine * factor_of(got_ref, half))


def intra_kernel(x_ref, write_ref, read_ref, log_ref, live_ref, skip_ref, out_ref):
    heads = log_ref.shape[0]
    tri, eye = tri_ones(GROUP)
    half = GROUP // 2
    live = column_of(live_ref[...], eye)[:, 0:1].astype(BF16)
    by_row = sums_by_row(log_ref[...], tri)
    by_col = sums_by_column(log_ref[...], tri)
    scores = contract(read_ref[...], write_ref[...], 1, 1)
    scores = jnp.where(tri > 0, scores, 0.0)
    lane = lax.broadcasted_iota(jnp.int32, (GROUP, 2 * HDIM), 1)
    for pair in range(heads // 2):
        cols = slice(pair * 2 * HDIM, (pair + 1) * 2 * HDIM)
        x = x_ref[:, cols] * live
        top = bottom = 0.0
        for k in range(2):
            h = 2 * pair + k
            mine = jnp.where((lane < HDIM) == (k == 0), x, jnp.zeros_like(x))
            row = by_row[h : h + 1, :]
            col = by_col[:, h : h + 1]
            gap = jnp.minimum(col[:half] - row[:, :half], 0.0)
            w = (scores[:half, :half] * jnp.exp(gap)).astype(BF16)
            top = top + contract(w, mine[:half], 1, 0)
            gap = jnp.minimum(col[half:] - row, 0.0)
            w = (scores[half:] * jnp.exp(gap)).astype(BF16)
            bottom = bottom + contract(w, mine, 1, 0)
        direct = skip_ref[:, cols] * x.astype(F32)
        out_ref[:half, cols] = top + direct[:half]
        out_ref[half:, cols] = bottom + direct[half:]


def gate_kernel(where_ref, direct_ref, mine_ref, other_ref, twin_ref, local_ref, dec_ref, read_ref, log_ref, start_ref, gate_ref, gain_ref, out_ref, sq_ref):
    heads = log_ref.shape[0]
    block = out_ref.shape[0]
    parts = GROUP // block
    rows = lax.broadcasted_iota(jnp.int32, (block, GROUP), 0) + pl.program_id(0) % parts * block
    tri = jnp.where(rows >= lax.broadcasted_iota(jnp.int32, (block, GROUP), 1), 1.0, 0.0).astype(BF16)
    spread = head_spread(heads)
    second = (pl.program_id(0) >= parts).astype(F32)
    core = (where_ref[3] == 1).astype(F32)
    mine, other = mine_ref[...].astype(F32), other_ref[...].astype(F32)
    chip = jnp.concatenate([(1.0 - core) * mine + core * other, (1.0 - core) * other + core * mine], 0)
    through = twin_ref[0:STATE, :].astype(F32) + factor_of(twin_ref, STATE) * chip
    arriving = ((1.0 - core) * chip + core * through).astype(BF16).astype(F32)
    carried = (1.0 - second + second * dec_ref[0:1, :]) * arriving + second * local_ref[...]
    crossed = contract(read_ref[...], carried.astype(BF16), 1, 0)
    fresh = 1.0 - start_ref[:, 0:1].astype(F32)
    reach = spread_wide(jnp.exp(sums_by_column(log_ref[...], tri)) * fresh, spread)
    gate = gate_ref[...].astype(F32)
    g = (direct_ref[...] + crossed * reach) * (gate / (1.0 + jnp.exp(-gate)))
    out_ref[...] = (g * gain_ref[...]).astype(BF16)
    squares = jnp.broadcast_to(jnp.sum(g * g, axis=1, keepdims=True), (block, 128))
    sq_ref[...] = jnp.transpose(squares)[0:8, :]


def assemble_kernel(where_ref, g_ref, *refs):
    own_ref, twin_ref, out_ref, w_ref = refs
    x_size, z_size, cores, rows, _ = w_ref.shape
    head, x_at, z_at, core = (where_ref[i] for i in range(4))

    def place(ref, base, x, k):
        way = jnp.where(k == 0, z_size - 1, 1)
        slots = [(z_at, k)]
        for turn in range(1, z_size // 2):
            z = (z_at + turn * way) % z_size
            slots += [(z, k), (z, 1 - k)]
        slots.append(((z_at + z_size // 2) % z_size, k))
        for slot, (z, block) in enumerate(slots):
            w_ref[x % x_size, z, block] = ref[base + slot]

    def one_x(turn, _):
        by = jnp.where(turn == 0, 0, jnp.where(turn == 1, x_size - 1, turn - 1))
        place(own_ref, turn * z_size, x_at + by, core)
        place(twin_ref, turn * z_size, x_at + by, 1 - core)

    lax.fori_loop(0, x_size, one_x, None)
    width = out_ref.shape[1]
    at = pl.multiple_of(((head + 2) % 4) * width, width)
    weights = w_ref[:, :, :, :, pl.ds(at, width)].reshape(g_ref.shape[1], width)
    out_ref[...] = contract(g_ref[...], weights, 1, 0).astype(BF16)


def product_kernel(head_ref, a_ref, w_ref, out_ref):
    weights = w_ref[...].reshape(a_ref.shape[1], w_ref.shape[-1])
    out_ref[0] = contract(a_ref[...], weights, 1, 0)


def down_kernel(where_ref, a_ref, w_ref, out_ref):
    block = a_ref.shape[1] // 4
    total = 0.0
    for x in range(4):
        weights = w_ref[:, (x - where_ref[1]) % 4].reshape(block, w_ref.shape[-1])
        total = total + contract(a_ref[:, x * block : (x + 1) * block], weights, 1, 0)
    out_ref[0] = total


def gained(ref, gain_ref, head, by):
    width = ref.shape[1]
    at = pl.multiple_of(((head + by) % 4) * width, width)
    return (ref[...].astype(F32) * gain_ref[:, pl.ds(at, width)]).astype(BF16)


def row_squares(ref):
    v = ref[...].astype(F32)
    return jnp.broadcast_to(jnp.sum(v * v, axis=1, keepdims=True), (ref.shape[0], 128))


def flat(ref):
    return ref[...].reshape(ref.shape[0] * ref.shape[1] * ref.shape[2], ref.shape[3])


def near_kernel(head_ref, own_ref, prev_ref, next_ref, gain_ref, w_own_ref, w_prev_ref, w_next_ref, acc_ref, sq_ref, x_ref):
    @pl.when(pl.program_id(0) == 0)
    def _():
        total = 0.0
        for slot, (ref, by) in enumerate([(own_ref, 0), (prev_ref, 3), (next_ref, 1)]):
            x_ref[slot] = gained(ref, gain_ref, head_ref[0], by)
            total = total + row_squares(ref)
        sq_ref[...] = total

    acc_ref[...] = sum(contract(x_ref[i], flat(ref), 1, 0) for i, ref in enumerate([w_own_ref, w_prev_ref, w_next_ref]))


def act_kernel(
    head_ref, far_ref, gain_ref, w_gate_ref, w_up_ref, gate_ref, up_ref, sq_ref, down_ref, act_ref, out_ref, x_ref, scale_ref, sum_ref
):
    step = pl.program_id(0)

    @pl.when(step == 0)
    def _():
        x_ref[...] = gained(far_ref, gain_ref, head_ref[0], 2)
        total = sq_ref[...] + row_squares(far_ref)
        scale_ref[...] = lax.rsqrt(total / (4 * far_ref.shape[1]) + EPS)
        sum_ref[...] = jnp.zeros_like(sum_ref)

    scale = scale_ref[:, 0:1]
    gate = (gate_ref[...] + contract(x_ref[...], flat(w_gate_ref), 1, 0)) * scale
    up = (up_ref[...] + contract(x_ref[...], flat(w_up_ref), 1, 0)) * scale
    act = (gate / (1.0 + jnp.exp(-gate)) * up).astype(BF16)
    act_ref[...] = act
    sum_ref[...] += contract(act, flat(down_ref), 1, 0)

    @pl.when(step == pl.num_programs(0) - 1)
    def _():
        out_ref[...] = sum_ref[...].astype(BF16)


def along_x(array, by, x_size, z_size):
    row = 2 * z_size
    return lax.ppermute(array, "ctx", [(i, (i + by * row) % (x_size * row)) for i in range(x_size * row)])


def moved(array, axis, x_size, z_size, far=1):
    pairs = []
    for x in range(x_size):
        for z in range(z_size):
            for core in range(2):
                by = far * (1 - 2 * core)
                to = {
                    "x": ((x + by) % x_size, z, core),
                    "z": (x, (z + by) % z_size, core),
                    "core": (x, z, 1 - core),
                }[axis]
                pairs.append(((x * z_size + z) * 2 + core, (to[0] * z_size + to[1]) * 2 + to[2]))
    return lax.ppermute(array, "ctx", pairs)


def sent(array, by):
    return lax.ppermute(array, "head", [(i, (i + by) % 4) for i in range(4)])


def scattered(far, parts):
    half = far.shape[0] // 2
    first, second = sent(far[:half], 1), sent(far[half:], -1)
    one, three, own = parts()
    one = jnp.concatenate([one[:half] + first.astype(F32), one[half:]], 0).astype(BF16)
    three = jnp.concatenate([three[:half], three[half:] + second.astype(F32)], 0).astype(BF16)
    return own + sent(one, 1).astype(F32) + sent(three, -1).astype(F32)


def shards(
    mixer_input,
    gate_input,
    write_vecs,
    read_vecs,
    log_decay,
    doc_start,
    live_mask,
    skip_gain,
    norm_gain,
    residual,
    out_weight,
    mlp_gain,
    gate_weight,
    up_weight,
    down_weight,
):
    tokens, inner = mixer_input.shape
    heads = log_decay.shape[0]
    peers = lax.axis_size("ctx")
    width = residual.shape[1]
    model = out_weight.shape[1]
    units = gate_weight.shape[1]
    in_rows, ff_rows, out_rows = gate_weight.shape[0], down_weight.shape[0], out_weight.shape[0]
    x_size = 4
    z_size = peers // (2 * x_size)

    packed = jnp.concatenate([jnp.concatenate([gate_weight, up_weight], 1), down_weight], 0)

    in_hbm = lambda a: pltpu.with_memory_space_constraint(a, pltpu.HBM)
    mixer_input, gate_input, write_vecs, read_vecs, log_decay = map(
        in_hbm, (mixer_input, gate_input, write_vecs, read_vecs, log_decay)
    )
    starts = doc_start.reshape(1, tokens)
    live = live_mask.reshape(1, tokens)
    skip = jnp.repeat(skip_gain, HDIM).reshape(1, inner)
    gain = norm_gain.reshape(1, inner)
    at = lax.axis_index("ctx")
    where = jnp.stack([lax.axis_index("head"), at // (2 * z_size), at // 2 % z_size, at % 2])

    entire = lambda shape: pl.BlockSpec(shape, lambda i: (0,) * len(shape))
    state_in = (mixer_input, write_vecs, log_decay, starts, live)
    state_out = (((STATE + 16, inner), BF16), ((STATE, inner), F32), ((8, inner), F32))
    payload, local_0, dec_0 = pl.pallas_call(
        state_kernel,
        grid=(1,),
        out_shape=tuple(jax.ShapeDtypeStruct(*o) for o in state_out),
        in_specs=[entire(a.shape) for a in state_in],
        out_specs=tuple(entire(o[0]) for o in state_out),
        compiler_params=params(),
        name="state",
    )(*state_in)

    def passed(array, by):
        return lax.ppermute(array, "ctx", [(i, i + by) for i in range(peers - by)])

    def joined(kernel, name, *arrays):
        return pl.pallas_call(
            kernel,
            out_shape=jax.ShapeDtypeStruct((STATE // 2 + 16, inner), BF16),
            in_specs=[pl.BlockSpec(memory_space=pltpu.SMEM if a.ndim == 1 else pltpu.VMEM) for a in arrays],
            out_specs=vmem(),
            compiler_params=params(),
            name=name,
        )(*arrays)

    by_group = pl.BlockSpec((GROUP, inner), lambda g: (g, 0))
    vecs = pl.BlockSpec((GROUP, STATE), lambda g: (g, 0))
    logs = pl.BlockSpec((heads, GROUP), lambda g: (0, g))
    flags = pl.BlockSpec((1, GROUP), lambda g: (0, g))
    whole = lambda a: pl.BlockSpec(a.shape, lambda g: (0,) * a.ndim)
    some = heads // 2
    direct = pl.pallas_call(
        intra_kernel,
        grid=(tokens // GROUP, 2),
        out_shape=jax.ShapeDtypeStruct((tokens, inner), F32),
        in_specs=[
            pl.BlockSpec((GROUP, inner // 2), lambda g, k: (g, k)),
            pl.BlockSpec((GROUP, STATE), lambda g, k: (g, 0)),
            pl.BlockSpec((GROUP, STATE), lambda g, k: (g, 0)),
            pl.BlockSpec((some, GROUP), lambda g, k: (k, g)),
            pl.BlockSpec((1, GROUP), lambda g, k: (0, g)),
            pl.BlockSpec((1, inner // 2), lambda g, k: (0, k)),
        ],
        out_specs=pl.BlockSpec((GROUP, inner // 2), lambda g, k: (g, k)),
        compiler_params=params(),
        name="intra",
    )(mixer_input, write_vecs, read_vecs, log_decay, live, skip)

    step = lambda array, axis, far=1: moved(array, axis, x_size, z_size, far)
    tie = lambda *arrays: lax.optimization_barrier(arrays)
    block = out_weight[None]
    row = lambda array, by: along_x(array, by, x_size, z_size)
    other, packed = tie(step(block, "core"), packed)
    beyond = row(packed, -1), step(packed, "x", 2), row(packed, 1)
    piece = jnp.concatenate([block, other], 0)
    reach = z_size // 2
    pieces = [step(piece, "z", far) for far in range(1, reach)] + [step(piece[:1], "z", reach)]
    *pieces, next_x, over_x, last_x, twin = tie(*pieces, *beyond, step(payload, "core"))
    beyond = next_x, over_x, last_x
    around_z = [list(range(x * 2 * z_size, (x + 1) * 2 * z_size)) for x in range(x_size)]
    weights = lax.all_gather(jnp.stack([packed, *beyond]), "ctx", axis=0, axis_index_groups=around_z)
    column = jnp.concatenate([block, *pieces], 0)
    chips = joined(pair_kernel, "pair", where, payload, twin)
    got, behind, ahead = tie(passed(chips, 2), row(column, 1), row(column, -1))
    chips = joined(join_kernel, "join", chips, got)
    ends = row(behind[:reach], 1), row(ahead[reach:], -1)
    got, *ends, direct = tie(passed(chips, 4), *ends, direct)
    chips = joined(join_kernel, "join", chips, got)
    own_out = jnp.concatenate([column, behind, ahead, *ends], 0)
    reached, twin_out = tie(passed(chips[: STATE // 2], 2), step(own_out, "core"))
    reached_twin = step(reached, "core")

    part = GROUP // 2
    by_part = pl.BlockSpec((part, inner), lambda i: (i, 0))
    gated, squares = pl.pallas_call(
        gate_kernel,
        grid=(tokens // part,),
        out_shape=(
            jax.ShapeDtypeStruct((tokens, inner), BF16),
            jax.ShapeDtypeStruct((8, tokens), F32),
        ),
        in_specs=[
            pl.BlockSpec(memory_space=pltpu.SMEM),
            by_part,
            whole(reached),
            whole(reached_twin),
            whole(twin),
            whole(local_0),
            whole(dec_0),
            pl.BlockSpec((part, STATE), lambda i: (i, 0)),
            pl.BlockSpec((heads, GROUP), lambda i: (0, i * part // GROUP)),
            pl.BlockSpec((1, GROUP), lambda i: (0, i * part // GROUP)),
            by_part,
            whole(gain),
        ],
        out_specs=(by_part, pl.BlockSpec((8, part), lambda i: (0, i))),
        compiler_params=params(),
        name="gating",
    )(where, direct, reached, reached_twin, twin, local_0, dec_0, read_vecs, log_decay, starts, gate_input, gain)
    mine = squares[0]
    total = mine + sent(mine, 1) + sent(mine, -1) + sent(mine, 2)
    row_scale = lax.rsqrt(total / INNER + EPS)

    def call(kernel, grid, ins, outs, scratch, name, *args):
        return pl.pallas_call(
            kernel,
            grid_spec=pltpu.PrefetchScalarGridSpec(
                num_scalar_prefetch=1,
                grid=grid,
                in_specs=[spec for spec, _ in ins],
                out_specs=[spec for spec, _ in outs],
                scratch_shapes=scratch,
            ),
            out_shape=[shape for _, shape in outs],
            compiler_params=params(),
            name=name,
        )(*args, *[array for _, array in ins])

    def fixed(array):
        return pl.BlockSpec(array.shape, lambda j, h: (0,) * array.ndim), array

    def new(shape, dtype, block=None, index=None):
        index = index or (lambda j, h: (0,) * len(shape))
        return pl.BlockSpec(block or shape, index), jax.ShapeDtypeStruct(shape, dtype)

    share = (tokens, width)
    grid_of_rows = (x_size, z_size, 2, out_rows, model)
    far, rows_in_order = call(
        assemble_kernel,
        (1,),
        [fixed(a) for a in (gated, own_out, twin_out)],
        [new(share, BF16), new(grid_of_rows, BF16)],
        [],
        "assemble",
        where,
    )

    def others(kernel, array, spec, name):
        (parts,) = call(
            kernel,
            (3,),
            [fixed(array), spec],
            [new((3, *share), F32, (1, *share), lambda j, h: (j, 0, 0))],
            [],
            name,
            where,
        )
        return parts[0], parts[1], parts[2]

    by_column = pl.BlockSpec((*grid_of_rows[:4], width), lambda j, h: (0, 0, 0, 0, (h[0] + jnp.where(j == 2, 0, 2 * j + 1)) % 4))
    summed = scattered(far, lambda: others(product_kernel, gated, (by_column, rows_in_order), "project"))
    hidden = (residual.astype(F32) + summed * row_scale[:, None]).astype(BF16)

    half = tokens // 2
    mlp_gains = mlp_gain.reshape(1, model)
    blocks = 2 * z_size
    narrow = units * 2 // 8

    def rows_of(by, block, index):
        return pl.BlockSpec((blocks, 1, in_rows, block), lambda j, h: (0, (h[0] + by - h[1]) % 4, 0, index(j))), weights

    wide = (tokens, 2 * units)
    hidden, weights = tie(hidden, weights)
    prev, following = sent(hidden, 1), sent(hidden, -1)
    prev, following = tie(prev, following)
    ends = sent(prev[:half], 1), sent(following[half:], -1)
    acc, squares = call(
        near_kernel,
        (8,),
        [
            fixed(hidden),
            fixed(prev),
            fixed(following),
            fixed(mlp_gains),
            rows_of(0, narrow, lambda j: j),
            rows_of(3, narrow, lambda j: j),
            rows_of(1, narrow, lambda j: j),
        ],
        [new(wide, F32, (tokens, narrow), lambda j, h: (0, j)), new((tokens, 128), F32)],
        [pltpu.VMEM((3, *share), BF16)],
        "mlp_near",
        where,
    )
    *ends, acc, squares = tie(*ends, acc, squares)
    acc = in_hbm(acc)
    ff_block = 256
    ff_steps = units // ff_block
    down_spec = pl.BlockSpec(
        (blocks, 1, ff_rows, width), lambda j, h: (0, (j - h[1]) % 4, in_rows // ff_rows, (h[0] + 2) % 4)
    )
    act, far = call(
        act_kernel,
        (ff_steps,),
        [
            fixed(jnp.concatenate(ends, 0)),
            fixed(mlp_gains),
            rows_of(2, ff_block, lambda j: j),
            rows_of(2, ff_block, lambda j: ff_steps + j),
            (pl.BlockSpec((tokens, ff_block), lambda j, h: (0, j)), acc),
            (pl.BlockSpec((tokens, ff_block), lambda j, h: (0, ff_steps + j)), acc),
            fixed(squares),
            (down_spec, weights),
        ],
        [new((tokens, units), BF16, (tokens, ff_block), lambda j, h: (0, j)), new(share, BF16)],
        [pltpu.VMEM(share, BF16), pltpu.VMEM((tokens, 128), F32), pltpu.VMEM(share, F32)],
        "mlp_act",
        where,
    )
    by_column = pl.BlockSpec(
        (blocks, x_size, ff_rows, width),
        lambda j, h: (0, 0, in_rows // ff_rows, (h[0] + jnp.where(j == 2, 0, 2 * j + 1)) % 4),
    )
    added = scattered(far, lambda: others(down_kernel, act, (by_column, weights), "mlp_down"))
    return (live_mask.astype(F32)[:, None] * (hidden.astype(F32) + added)).astype(BF16)


def solution(mesh):
    return jax.shard_map(
        shards,
        mesh=mesh,
        in_specs=(
            P("ctx", "head"),
            P("ctx", "head"),
            P("ctx", None),
            P("ctx", None),
            P("head", "ctx"),
            P("ctx"),
            P("ctx"),
            P("head"),
            P("head"),
            P("ctx", "head"),
            P(("head", "ctx"), None),
            P(),
            P("ctx", "head"),
            P("ctx", "head"),
            P(("head", "ctx"), None),
        ),
        out_specs=P("ctx", "head"),
        check_vma=False,
    )
```

```python
import jax
import jax.numpy as jnp
from jax import lax
from jax.experimental import pallas as pl
from jax.experimental.pallas import tpu as pltpu
from jax.sharding import PartitionSpec as P

HDIM = 64
STATE = 128
GROUP = 256
DOC_GROUPS = 16
INNER = 4096
EPS = 1e-05
F32 = jnp.float32
BF16 = jnp.bfloat16


def params(mib=28):
    return pltpu.CompilerParams(vmem_limit_bytes=mib * 1024 * 1024)


def vmem():
    return pl.BlockSpec(memory_space=pltpu.VMEM)


def contract(a, b, da, db):
    return lax.dot_general(a, b, (((da,), (db,)), ((), ())), preferred_element_type=F32)


def split2(v):
    hi = v.astype(BF16)
    return hi, (v - hi.astype(F32)).astype(BF16)


def split3(v):
    hi = v.astype(BF16)
    rest = v - hi.astype(F32)
    mid = rest.astype(BF16)
    return hi, mid, (rest - mid.astype(F32)).astype(BF16)


def tri_ones(n):
    rows = lax.broadcasted_iota(jnp.int32, (n, n), 0)
    cols = lax.broadcasted_iota(jnp.int32, (n, n), 1)
    return jnp.where(rows >= cols, 1.0, 0.0).astype(BF16), jnp.where(rows == cols, 1.0, 0.0).astype(BF16)


def head_spread(heads):
    rows = lax.broadcasted_iota(jnp.int32, (heads, heads * HDIM), 0)
    cols = lax.broadcasted_iota(jnp.int32, (heads, heads * HDIM), 1)
    return jnp.where(cols // HDIM == rows, 1.0, 0.0).astype(BF16)


def spread_wide(cols, spread):
    hi, lo = split2(cols)
    return contract(hi, spread, 1, 0) + contract(lo, spread, 1, 0)


def sums_by_row(log_group, tri):
    return sum(contract(part, tri, 1, 1) for part in split3(log_group))


def sums_by_column(log_group, tri):
    return sum(contract(tri, part, 1, 1) for part in split3(log_group))


def column_of(row, eye):
    return contract(eye, jnp.broadcast_to(row.astype(F32), (16, row.shape[1])).astype(BF16), 1, 1)


def state_kernel(x_ref, write_ref, log_ref, start_ref, live_ref, pay_ref, local_ref, dec_ref):
    heads = log_ref.shape[0]
    tri, eye = tri_ones(GROUP)
    spread = head_spread(heads)
    locals_, decays = [], []
    for g in range(2):
        rows = slice(g * GROUP, (g + 1) * GROUP)
        sums = sums_by_column(log_ref[:, rows], tri)
        last = sums[GROUP - 1 : GROUP, :]
        live = column_of(live_ref[:, rows], eye)
        tail = spread_wide(jnp.exp(last - sums) * live, spread)
        scaled = (x_ref[rows, :].astype(F32) * tail).astype(BF16)
        locals_.append(contract(write_ref[rows, :], scaled, 0, 0))
        fresh = 1.0 - start_ref[:, g * GROUP : g * GROUP + 1].astype(F32)
        end = jnp.broadcast_to(jnp.exp(last) * fresh, (16, heads))
        decays.append(sum(contract(part, spread, 1, 0) for part in split3(end)))
    state = decays[1][0:1] * locals_[0] + locals_[1]
    pay_ref[0:STATE, :] = state.astype(BF16)
    pay_ref[STATE : STATE + 16, :] = factor_rows((decays[0] * decays[1])[0:1])
    local_ref[...] = locals_[0]
    dec_ref[...] = decays[0][0:8]


def stack_kernel(*refs):
    at = 0
    for ref in refs[:-1]:
        refs[-1][at : at + ref.shape[0]] = ref[...]
        at += ref.shape[0]


def factor_of(ref, at):
    tail = ref[at : at + 16, :].astype(F32)
    return tail[0:1] + tail[1:2] + tail[2:3]


def factor_rows(factor):
    both = jnp.broadcast_to(factor, (16, factor.shape[1]))
    hi, mid, low = split3(both)
    row = lax.broadcasted_iota(jnp.int32, both.shape, 0)
    packed = jnp.where(row == 0, hi.astype(F32), jnp.where(row == 1, mid.astype(F32), low.astype(F32)))
    return packed.astype(BF16)


def pair_kernel(where_ref, mine_ref, twin_ref, out_ref):
    core = where_ref[3]
    half = STATE // 2
    at = pl.multiple_of(core * half, half)
    mine, twin = factor_of(mine_ref, STATE), factor_of(twin_ref, STATE)
    own = mine_ref[pl.ds(at, half), :].astype(F32)
    got = twin_ref[pl.ds(at, half), :].astype(F32)
    second = (core == 1).astype(F32)
    state = second * (own + mine * got) + (1.0 - second) * (got + twin * own)
    out_ref[0:half, :] = state.astype(BF16)
    out_ref[half : half + 16, :] = factor_rows(mine * twin)


def join_kernel(own_ref, got_ref, out_ref):
    half = STATE // 2
    mine = factor_of(own_ref, half)
    state = own_ref[0:half, :].astype(F32) + mine * got_ref[0:half, :].astype(F32)
    out_ref[0:half, :] = state.astype(BF16)
    out_ref[half : half + 16, :] = factor_rows(mine * factor_of(got_ref, half))


def intra_kernel(x_ref, write_ref, read_ref, log_ref, live_ref, skip_ref, out_ref):
    heads = log_ref.shape[0]
    tri, eye = tri_ones(GROUP)
    half = GROUP // 2
    live = column_of(live_ref[...], eye)[:, 0:1].astype(BF16)
    by_row = sums_by_row(log_ref[...], tri)
    by_col = sums_by_column(log_ref[...], tri)
    scores = contract(read_ref[...], write_ref[...], 1, 1)
    scores = jnp.where(tri > 0, scores, 0.0)
    lane = lax.broadcasted_iota(jnp.int32, (GROUP, 2 * HDIM), 1)
    for pair in range(heads // 2):
        cols = slice(pair * 2 * HDIM, (pair + 1) * 2 * HDIM)
        x = x_ref[:, cols] * live
        top = bottom = 0.0
        for k in range(2):
            h = 2 * pair + k
            mine = jnp.where((lane < HDIM) == (k == 0), x, jnp.zeros_like(x))
            row = by_row[h : h + 1, :]
            col = by_col[:, h : h + 1]
            gap = jnp.minimum(col[:half] - row[:, :half], 0.0)
            w = (scores[:half, :half] * jnp.exp(gap)).astype(BF16)
            top = top + contract(w, mine[:half], 1, 0)
            gap = jnp.minimum(col[half:] - row, 0.0)
            w = (scores[half:] * jnp.exp(gap)).astype(BF16)
            bottom = bottom + contract(w, mine, 1, 0)
        direct = skip_ref[:, cols] * x.astype(F32)
        out_ref[:half, cols] = top + direct[:half]
        out_ref[half:, cols] = bottom + direct[half:]


def gate_kernel(where_ref, direct_ref, mine_ref, other_ref, twin_ref, local_ref, dec_ref, read_ref, log_ref, start_ref, gate_ref, gain_ref, out_ref, sq_ref):
    heads = log_ref.shape[0]
    block = out_ref.shape[0]
    parts = GROUP // block
    rows = lax.broadcasted_iota(jnp.int32, (block, GROUP), 0) + pl.program_id(0) % parts * block
    tri = jnp.where(rows >= lax.broadcasted_iota(jnp.int32, (block, GROUP), 1), 1.0, 0.0).astype(BF16)
    spread = head_spread(heads)
    second = (pl.program_id(0) >= parts).astype(F32)
    core = (where_ref[3] == 1).astype(F32)
    mine, other = mine_ref[...].astype(F32), other_ref[...].astype(F32)
    chip = jnp.concatenate([(1.0 - core) * mine + core * other, (1.0 - core) * other + core * mine], 0)
    through = twin_ref[0:STATE, :].astype(F32) + factor_of(twin_ref, STATE) * chip
    arriving = ((1.0 - core) * chip + core * through).astype(BF16).astype(F32)
    carried = (1.0 - second + second * dec_ref[0:1, :]) * arriving + second * local_ref[...]
    crossed = contract(read_ref[...], carried.astype(BF16), 1, 0)
    fresh = 1.0 - start_ref[:, 0:1].astype(F32)
    reach = spread_wide(jnp.exp(sums_by_column(log_ref[...], tri)) * fresh, spread)
    gate = gate_ref[...].astype(F32)
    g = (direct_ref[...] + crossed * reach) * (gate / (1.0 + jnp.exp(-gate)))
    out_ref[...] = (g * gain_ref[...]).astype(BF16)
    squares = jnp.broadcast_to(jnp.sum(g * g, axis=1, keepdims=True), (block, 128))
    sq_ref[...] = jnp.transpose(squares)[0:8, :]


def assemble_kernel(where_ref, g_ref, *refs):
    own_ref, twin_ref, out_ref, w_ref = refs
    x_size, z_size, cores, rows, _ = w_ref.shape
    head, x_at, z_at, core = (where_ref[i] for i in range(4))

    def place(ref, base, x, k):
        way = jnp.where(k == 0, z_size - 1, 1)
        slots = [(z_at, k)]
        for turn in range(1, z_size // 2):
            z = (z_at + turn * way) % z_size
            slots += [(z, k), (z, 1 - k)]
        slots.append(((z_at + z_size // 2) % z_size, k))
        for slot, (z, block) in enumerate(slots):
            w_ref[x % x_size, z, block] = ref[base + slot]

    def one_x(turn, _):
        by = jnp.where(turn == 0, 0, jnp.where(turn == 1, x_size - 1, turn - 1))
        place(own_ref, turn * z_size, x_at + by, core)
        place(twin_ref, turn * z_size, x_at + by, 1 - core)

    lax.fori_loop(0, x_size, one_x, None)
    width = out_ref.shape[1]
    at = pl.multiple_of(((head + 2) % 4) * width, width)
    weights = w_ref[:, :, :, :, pl.ds(at, width)].reshape(g_ref.shape[1], width)
    out_ref[...] = contract(g_ref[...], weights, 1, 0).astype(BF16)


def product_kernel(head_ref, a_ref, w_ref, out_ref):
    weights = w_ref[...].reshape(a_ref.shape[1], w_ref.shape[-1])
    out_ref[0] = contract(a_ref[...], weights, 1, 0)


def down_kernel(where_ref, a_ref, w_ref, out_ref):
    block = a_ref.shape[1] // 4
    total = 0.0
    for x in range(4):
        weights = w_ref[:, (x - where_ref[1]) % 4].reshape(block, w_ref.shape[-1])
        total = total + contract(a_ref[:, x * block : (x + 1) * block], weights, 1, 0)
    out_ref[0] = total


def gained(ref, gain_ref, head, by):
    width = ref.shape[1]
    at = pl.multiple_of(((head + by) % 4) * width, width)
    return (ref[...].astype(F32) * gain_ref[:, pl.ds(at, width)]).astype(BF16)


def row_squares(ref):
    v = ref[...].astype(F32)
    return jnp.broadcast_to(jnp.sum(v * v, axis=1, keepdims=True), (ref.shape[0], 128))


def flat(ref):
    return ref[...].reshape(ref.shape[0] * ref.shape[1] * ref.shape[2], ref.shape[3])


def near_kernel(head_ref, own_ref, prev_ref, next_ref, gain_ref, w_own_ref, w_prev_ref, w_next_ref, acc_ref, sq_ref, x_ref):
    @pl.when(pl.program_id(0) == 0)
    def _():
        total = 0.0
        for slot, (ref, by) in enumerate([(own_ref, 0), (prev_ref, 3), (next_ref, 1)]):
            x_ref[slot] = gained(ref, gain_ref, head_ref[0], by)
            total = total + row_squares(ref)
        sq_ref[...] = total

    acc_ref[...] = sum(contract(x_ref[i], flat(ref), 1, 0) for i, ref in enumerate([w_own_ref, w_prev_ref, w_next_ref]))


def act_kernel(
    head_ref, far_ref, gain_ref, w_gate_ref, w_up_ref, acc_ref, sq_ref, down_ref, act_ref, out_ref, x_ref, scale_ref, sum_ref
):
    step = pl.program_id(0)

    @pl.when(step == 0)
    def _():
        x_ref[...] = gained(far_ref, gain_ref, head_ref[0], 2)
        total = sq_ref[...] + row_squares(far_ref)
        scale_ref[...] = lax.rsqrt(total / (4 * far_ref.shape[1]) + EPS)
        sum_ref[...] = jnp.zeros_like(sum_ref)

    scale = scale_ref[:, 0:1]
    block = w_up_ref.shape[-1]
    gate = (acc_ref[:, :block] + contract(x_ref[...], flat(w_gate_ref), 1, 0)) * scale
    up = (acc_ref[:, block:] + contract(x_ref[...], flat(w_up_ref), 1, 0)) * scale
    act = (gate / (1.0 + jnp.exp(-gate)) * up).astype(BF16)
    act_ref[...] = act
    sum_ref[...] += contract(act, flat(down_ref), 1, 0)

    @pl.when(step == pl.num_programs(0) - 1)
    def _():
        out_ref[...] = sum_ref[...].astype(BF16)


def along_x(array, by, x_size, z_size):
    row = 2 * z_size
    return lax.ppermute(array, "ctx", [(i, (i + by * row) % (x_size * row)) for i in range(x_size * row)])


def moved(array, axis, x_size, z_size, far=1):
    pairs = []
    for x in range(x_size):
        for z in range(z_size):
            for core in range(2):
                by = far * (1 - 2 * core)
                to = {
                    "x": ((x + by) % x_size, z, core),
                    "z": (x, (z + by) % z_size, core),
                    "core": (x, z, 1 - core),
                }[axis]
                pairs.append(((x * z_size + z) * 2 + core, (to[0] * z_size + to[1]) * 2 + to[2]))
    return lax.ppermute(array, "ctx", pairs)


def sent(array, by):
    return lax.ppermute(array, "head", [(i, (i + by) % 4) for i in range(4)])


def scattered(far, parts):
    half = far.shape[0] // 2
    first, second = sent(far[:half], 1), sent(far[half:], -1)
    one, three, own = parts()
    one = jnp.concatenate([one[:half] + first.astype(F32), one[half:]], 0).astype(BF16)
    three = jnp.concatenate([three[:half], three[half:] + second.astype(F32)], 0).astype(BF16)
    return own + sent(one, 1).astype(F32) + sent(three, -1).astype(F32)


def shards(
    mixer_input,
    gate_input,
    write_vecs,
    read_vecs,
    log_decay,
    doc_start,
    live_mask,
    skip_gain,
    norm_gain,
    residual,
    out_weight,
    mlp_gain,
    gate_weight,
    up_weight,
    down_weight,
):
    tokens, inner = mixer_input.shape
    heads = log_decay.shape[0]
    peers = lax.axis_size("ctx")
    width = residual.shape[1]
    model = out_weight.shape[1]
    units = gate_weight.shape[1]
    in_rows, ff_rows, out_rows = gate_weight.shape[0], down_weight.shape[0], out_weight.shape[0]
    x_size = 4
    z_size = peers // (2 * x_size)

    packed = jnp.concatenate([jnp.concatenate([gate_weight, up_weight], 1), down_weight], 0)

    in_hbm = lambda a: pltpu.with_memory_space_constraint(a, pltpu.HBM)
    mixer_input, gate_input, write_vecs, read_vecs, log_decay = map(
        in_hbm, (mixer_input, gate_input, write_vecs, read_vecs, log_decay)
    )
    starts = doc_start.reshape(1, tokens)
    live = live_mask.reshape(1, tokens)
    skip = jnp.repeat(skip_gain, HDIM).reshape(1, inner)
    gain = norm_gain.reshape(1, inner)
    at = lax.axis_index("ctx")
    where = jnp.stack([lax.axis_index("head"), at // (2 * z_size), at // 2 % z_size, at % 2])

    entire = lambda shape: pl.BlockSpec(shape, lambda i: (0,) * len(shape))
    state_in = (mixer_input, write_vecs, log_decay, starts, live)
    state_out = (((STATE + 16, inner), BF16), ((STATE, inner), F32), ((8, inner), F32))
    payload, local_0, dec_0 = pl.pallas_call(
        state_kernel,
        grid=(1,),
        out_shape=tuple(jax.ShapeDtypeStruct(*o) for o in state_out),
        in_specs=[entire(a.shape) for a in state_in],
        out_specs=tuple(entire(o[0]) for o in state_out),
        compiler_params=params(),
        name="state",
    )(*state_in)

    def passed(array, by):
        return lax.ppermute(array, "ctx", [(i, i + by) for i in range(peers - by)])

    def joined(kernel, name, *arrays):
        return pl.pallas_call(
            kernel,
            out_shape=jax.ShapeDtypeStruct((STATE // 2 + 16, inner), BF16),
            in_specs=[pl.BlockSpec(memory_space=pltpu.SMEM if a.ndim == 1 else pltpu.VMEM) for a in arrays],
            out_specs=vmem(),
            compiler_params=params(),
            name=name,
        )(*arrays)

    by_group = pl.BlockSpec((GROUP, inner), lambda g: (g, 0))
    vecs = pl.BlockSpec((GROUP, STATE), lambda g: (g, 0))
    logs = pl.BlockSpec((heads, GROUP), lambda g: (0, g))
    flags = pl.BlockSpec((1, GROUP), lambda g: (0, g))
    whole = lambda a: pl.BlockSpec(a.shape, lambda g: (0,) * a.ndim)
    some = heads // 2
    direct = pl.pallas_call(
        intra_kernel,
        grid=(tokens // GROUP, 2),
        out_shape=jax.ShapeDtypeStruct((tokens, inner), F32),
        in_specs=[
            pl.BlockSpec((GROUP, inner // 2), lambda g, k: (g, k)),
            pl.BlockSpec((GROUP, STATE), lambda g, k: (g, 0)),
            pl.BlockSpec((GROUP, STATE), lambda g, k: (g, 0)),
            pl.BlockSpec((some, GROUP), lambda g, k: (k, g)),
            pl.BlockSpec((1, GROUP), lambda g, k: (0, g)),
            pl.BlockSpec((1, inner // 2), lambda g, k: (0, k)),
        ],
        out_specs=pl.BlockSpec((GROUP, inner // 2), lambda g, k: (g, k)),
        compiler_params=params(),
        name="intra",
    )(mixer_input, write_vecs, read_vecs, log_decay, live, skip)

    step = lambda array, axis, far=1: moved(array, axis, x_size, z_size, far)
    tie = lambda *arrays: lax.optimization_barrier(arrays)
    block = out_weight[None]
    row = lambda array, by: along_x(array, by, x_size, z_size)
    other, packed = tie(step(block, "core"), packed)
    beyond = row(packed, -1), step(packed, "x", 2), row(packed, 1)
    piece = jnp.concatenate([block, other], 0)
    reach = z_size // 2
    first, *pieces = [step(piece, "z", far) for far in range(1, reach)] + [step(piece[:1], "z", reach)]
    twin = step(payload, "core")
    first, twin, next_x, over_x, last_x = tie(first, twin, *beyond)
    chips = joined(pair_kernel, "pair", where, payload, twin)
    got = passed(chips, 2)
    around_z = [list(range(x * 2 * z_size, (x + 1) * 2 * z_size)) for x in range(x_size)]
    weights = lax.all_gather(jnp.stack([packed, next_x, over_x, last_x]), "ctx", axis=0, axis_index_groups=around_z)
    *pieces, got = tie(*pieces, got)
    chips, first = tie(joined(join_kernel, "join", chips, got), first)
    column_parts = [block, first, *pieces]
    column = pl.pallas_call(
        stack_kernel,
        out_shape=jax.ShapeDtypeStruct((z_size, out_rows, model), BF16),
        in_specs=[vmem()] * len(column_parts),
        out_specs=vmem(),
        compiler_params=params(),
        name="column",
    )(*column_parts)
    got, behind, ahead, direct = tie(passed(chips, 4), row(column, 1), row(column, -1), direct)
    chips, behind, ahead = tie(joined(join_kernel, "join", chips, got), behind, ahead)
    reached = passed(chips[: STATE // 2], 2)
    ends = row(behind[:reach], 1), row(ahead[reach:], -1)
    *ends, reached = tie(*ends, reached)
    own_out = jnp.concatenate([column, behind, ahead, *ends], 0)
    twin_out = step(own_out, "core")
    reached_twin = step(reached, "core")

    part = GROUP // 2
    by_part = pl.BlockSpec((part, inner), lambda i: (i, 0))
    gated, squares = pl.pallas_call(
        gate_kernel,
        grid=(tokens // part,),
        out_shape=(
            jax.ShapeDtypeStruct((tokens, inner), BF16),
            jax.ShapeDtypeStruct((8, tokens), F32),
        ),
        in_specs=[
            pl.BlockSpec(memory_space=pltpu.SMEM),
            by_part,
            whole(reached),
            whole(reached_twin),
            whole(twin),
            whole(local_0),
            whole(dec_0),
            pl.BlockSpec((part, STATE), lambda i: (i, 0)),
            pl.BlockSpec((heads, GROUP), lambda i: (0, i * part // GROUP)),
            pl.BlockSpec((1, GROUP), lambda i: (0, i * part // GROUP)),
            by_part,
            whole(gain),
        ],
        out_specs=(by_part, pl.BlockSpec((8, part), lambda i: (0, i))),
        compiler_params=params(),
        name="gating",
    )(where, direct, reached, reached_twin, twin, local_0, dec_0, read_vecs, log_decay, starts, gate_input, gain)
    mine = squares[0]
    total = mine + sent(mine, 1) + sent(mine, -1) + sent(mine, 2)
    row_scale = lax.rsqrt(total / INNER + EPS)

    def call(kernel, grid, ins, outs, scratch, name, *args):
        return pl.pallas_call(
            kernel,
            grid_spec=pltpu.PrefetchScalarGridSpec(
                num_scalar_prefetch=1,
                grid=grid,
                in_specs=[spec for spec, _ in ins],
                out_specs=[spec for spec, _ in outs],
                scratch_shapes=scratch,
            ),
            out_shape=[shape for _, shape in outs],
            compiler_params=params(),
            name=name,
        )(*args, *[array for _, array in ins])

    def fixed(array):
        return pl.BlockSpec(array.shape, lambda j, h: (0,) * array.ndim), array

    def new(shape, dtype, block=None, index=None):
        index = index or (lambda j, h: (0,) * len(shape))
        return pl.BlockSpec(block or shape, index), jax.ShapeDtypeStruct(shape, dtype)

    share = (tokens, width)
    grid_of_rows = (x_size, z_size, 2, out_rows, model)
    far, rows_in_order = call(
        assemble_kernel,
        (1,),
        [fixed(a) for a in (gated, own_out, twin_out)],
        [new(share, BF16), new(grid_of_rows, BF16)],
        [],
        "assemble",
        where,
    )

    def others(kernel, array, spec, name):
        (parts,) = call(
            kernel,
            (3,),
            [fixed(array), spec],
            [new((3, *share), F32, (1, *share), lambda j, h: (j, 0, 0))],
            [],
            name,
            where,
        )
        return parts[0], parts[1], parts[2]

    by_column = pl.BlockSpec((*grid_of_rows[:4], width), lambda j, h: (0, 0, 0, 0, (h[0] + jnp.where(j == 2, 0, 2 * j + 1)) % 4))
    summed = scattered(far, lambda: others(product_kernel, gated, (by_column, rows_in_order), "project"))
    hidden = (residual.astype(F32) + summed * row_scale[:, None]).astype(BF16)

    half = tokens // 2
    mlp_gains = mlp_gain.reshape(1, model)
    blocks = 2 * z_size

    def rows_of(by, block, index):
        return pl.BlockSpec((blocks, 1, in_rows, block), lambda j, h: (0, (h[0] + by - h[1]) % 4, 0, index(j))), weights

    wide = (tokens, 2 * units)
    hidden, weights = tie(hidden, weights)
    weights = in_hbm(weights)
    prev, following = sent(hidden, 1), sent(hidden, -1)
    prev, following = tie(prev, following)
    ends = sent(prev[:half], 1), sent(following[half:], -1)
    ff_block = 256
    ff_steps = units // ff_block
    paired = lambda j: j % 2 * ff_steps + j // 2
    acc, squares = call(
        near_kernel,
        (2 * ff_steps,),
        [
            fixed(hidden),
            fixed(prev),
            fixed(following),
            fixed(mlp_gains),
            rows_of(0, ff_block, paired),
            rows_of(3, ff_block, paired),
            rows_of(1, ff_block, paired),
        ],
        [new(wide, F32, (tokens, ff_block), lambda j, h: (0, j)), new((tokens, 128), F32)],
        [pltpu.VMEM((3, *share), BF16)],
        "mlp_near",
        where,
    )
    down_spec = pl.BlockSpec(
        (blocks, 1, ff_rows, width), lambda j, h: (0, (j - h[1]) % 4, in_rows // ff_rows, (h[0] + 2) % 4)
    )
    act, far = call(
        act_kernel,
        (ff_steps,),
        [
            fixed(jnp.concatenate(ends, 0)),
            fixed(mlp_gains),
            rows_of(2, ff_block, lambda j: j),
            rows_of(2, ff_block, lambda j: ff_steps + j),
            (pl.BlockSpec((tokens, 2 * ff_block), lambda j, h: (0, j)), acc),
            fixed(squares),
            (down_spec, weights),
        ],
        [new((tokens, units), BF16, (tokens, ff_block), lambda j, h: (0, j)), new(share, BF16)],
        [pltpu.VMEM(share, BF16), pltpu.VMEM((tokens, 128), F32), pltpu.VMEM(share, F32)],
        "mlp_act",
        where,
    )
    by_column = pl.BlockSpec(
        (blocks, x_size, ff_rows, width),
        lambda j, h: (0, 0, in_rows // ff_rows, (h[0] + jnp.where(j == 2, 0, 2 * j + 1)) % 4),
    )
    added = scattered(far, lambda: others(down_kernel, act, (by_column, weights), "mlp_down"))
    return (live_mask.astype(F32)[:, None] * (hidden.astype(F32) + added)).astype(BF16)


def solution(mesh):
    return jax.shard_map(
        shards,
        mesh=mesh,
        in_specs=(
            P("ctx", "head"),
            P("ctx", "head"),
            P("ctx", None),
            P("ctx", None),
            P("head", "ctx"),
            P("ctx"),
            P("ctx"),
            P("head"),
            P("head"),
            P("ctx", "head"),
            P(("head", "ctx"), None),
            P(),
            P("ctx", "head"),
            P("ctx", "head"),
            P(("head", "ctx"), None),
        ),
        out_specs=P("ctx", "head"),
        check_vma=False,
    )
```

```python
import jax
import jax.numpy as jnp
from jax import lax
from jax.experimental import pallas as pl
from jax.experimental.pallas import tpu as pltpu
from jax.sharding import PartitionSpec as P

HDIM = 64
STATE = 128
GROUP = 256
DOC_GROUPS = 16
INNER = 4096
EPS = 1e-05
F32 = jnp.float32
BF16 = jnp.bfloat16


def params(mib=28):
    return pltpu.CompilerParams(vmem_limit_bytes=mib * 1024 * 1024)


def vmem():
    return pl.BlockSpec(memory_space=pltpu.VMEM)


def contract(a, b, da, db):
    return lax.dot_general(a, b, (((da,), (db,)), ((), ())), preferred_element_type=F32)


def split2(v):
    hi = v.astype(BF16)
    return hi, (v - hi.astype(F32)).astype(BF16)


def split3(v):
    hi = v.astype(BF16)
    rest = v - hi.astype(F32)
    mid = rest.astype(BF16)
    return hi, mid, (rest - mid.astype(F32)).astype(BF16)


def tri_ones(n):
    rows = lax.broadcasted_iota(jnp.int32, (n, n), 0)
    cols = lax.broadcasted_iota(jnp.int32, (n, n), 1)
    return jnp.where(rows >= cols, 1.0, 0.0).astype(BF16), jnp.where(rows == cols, 1.0, 0.0).astype(BF16)


def head_spread(heads):
    rows = lax.broadcasted_iota(jnp.int32, (heads, heads * HDIM), 0)
    cols = lax.broadcasted_iota(jnp.int32, (heads, heads * HDIM), 1)
    return jnp.where(cols // HDIM == rows, 1.0, 0.0).astype(BF16)


def spread_wide(cols, spread):
    hi, lo = split2(cols)
    return contract(hi, spread, 1, 0) + contract(lo, spread, 1, 0)


def sums_by_row(log_group, tri):
    return sum(contract(part, tri, 1, 1) for part in split3(log_group))


def sums_by_column(log_group, tri):
    return sum(contract(tri, part, 1, 1) for part in split3(log_group))


def column_of(row, eye):
    return contract(eye, jnp.broadcast_to(row.astype(F32), (16, row.shape[1])).astype(BF16), 1, 1)


def state_kernel(x_ref, write_ref, log_ref, start_ref, live_ref, pay_ref, local_ref, dec_ref):
    heads = log_ref.shape[0]
    tri, eye = tri_ones(GROUP)
    spread = head_spread(heads)
    locals_, decays = [], []
    for g in range(2):
        rows = slice(g * GROUP, (g + 1) * GROUP)
        sums = sums_by_column(log_ref[:, rows], tri)
        last = sums[GROUP - 1 : GROUP, :]
        live = column_of(live_ref[:, rows], eye)
        tail = spread_wide(jnp.exp(last - sums) * live, spread)
        scaled = (x_ref[rows, :].astype(F32) * tail).astype(BF16)
        locals_.append(contract(write_ref[rows, :], scaled, 0, 0))
        fresh = 1.0 - start_ref[:, g * GROUP : g * GROUP + 1].astype(F32)
        end = jnp.broadcast_to(jnp.exp(last) * fresh, (16, heads))
        decays.append(sum(contract(part, spread, 1, 0) for part in split3(end)))
    state = decays[1][0:1] * locals_[0] + locals_[1]
    pay_ref[0:STATE, :] = state.astype(BF16)
    pay_ref[STATE : STATE + 16, :] = factor_rows((decays[0] * decays[1])[0:1])
    local_ref[...] = locals_[0]
    dec_ref[...] = decays[0][0:8]


def stack_kernel(*refs):
    at = 0
    for ref in refs[:-1]:
        refs[-1][at : at + ref.shape[0]] = ref[...]
        at += ref.shape[0]


def factor_of(ref, at):
    tail = ref[at : at + 16, :].astype(F32)
    return tail[0:1] + tail[1:2] + tail[2:3]


def factor_rows(factor):
    both = jnp.broadcast_to(factor, (16, factor.shape[1]))
    hi, mid, low = split3(both)
    row = lax.broadcasted_iota(jnp.int32, both.shape, 0)
    packed = jnp.where(row == 0, hi.astype(F32), jnp.where(row == 1, mid.astype(F32), low.astype(F32)))
    return packed.astype(BF16)


def pair_kernel(where_ref, mine_ref, twin_ref, out_ref):
    core = where_ref[3]
    half = STATE // 2
    at = pl.multiple_of(core * half, half)
    mine, twin = factor_of(mine_ref, STATE), factor_of(twin_ref, STATE)
    own = mine_ref[pl.ds(at, half), :].astype(F32)
    got = twin_ref[pl.ds(at, half), :].astype(F32)
    second = (core == 1).astype(F32)
    state = second * (own + mine * got) + (1.0 - second) * (got + twin * own)
    out_ref[0:half, :] = state.astype(BF16)
    out_ref[half : half + 16, :] = factor_rows(mine * twin)


def join_kernel(own_ref, got_ref, out_ref):
    half = STATE // 2
    mine = factor_of(own_ref, half)
    state = own_ref[0:half, :].astype(F32) + mine * got_ref[0:half, :].astype(F32)
    out_ref[0:half, :] = state.astype(BF16)
    out_ref[half : half + 16, :] = factor_rows(mine * factor_of(got_ref, half))


def intra_kernel(x_ref, write_ref, read_ref, log_ref, live_ref, skip_ref, out_ref):
    heads = log_ref.shape[0]
    tri, eye = tri_ones(GROUP)
    half = GROUP // 2
    live = column_of(live_ref[...], eye)[:, 0:1].astype(BF16)
    by_row = sums_by_row(log_ref[...], tri)
    by_col = sums_by_column(log_ref[...], tri)
    scores = contract(read_ref[...], write_ref[...], 1, 1)
    scores = jnp.where(tri > 0, scores, 0.0)
    lane = lax.broadcasted_iota(jnp.int32, (GROUP, 2 * HDIM), 1)
    for pair in range(heads // 2):
        cols = slice(pair * 2 * HDIM, (pair + 1) * 2 * HDIM)
        x = x_ref[:, cols] * live
        top = bottom = 0.0
        for k in range(2):
            h = 2 * pair + k
            mine = jnp.where((lane < HDIM) == (k == 0), x, jnp.zeros_like(x))
            row = by_row[h : h + 1, :]
            col = by_col[:, h : h + 1]
            gap = jnp.minimum(col[:half] - row[:, :half], 0.0)
            w = (scores[:half, :half] * jnp.exp(gap)).astype(BF16)
            top = top + contract(w, mine[:half], 1, 0)
            gap = jnp.minimum(col[half:] - row, 0.0)
            w = (scores[half:] * jnp.exp(gap)).astype(BF16)
            bottom = bottom + contract(w, mine, 1, 0)
        direct = skip_ref[:, cols] * x.astype(F32)
        out_ref[:half, cols] = top + direct[:half]
        out_ref[half:, cols] = bottom + direct[half:]


def gate_kernel(where_ref, direct_ref, mine_ref, other_ref, twin_ref, local_ref, dec_ref, read_ref, log_ref, start_ref, gate_ref, gain_ref, out_ref, sq_ref):
    heads = log_ref.shape[0]
    block = out_ref.shape[0]
    parts = GROUP // block
    rows = lax.broadcasted_iota(jnp.int32, (block, GROUP), 0) + pl.program_id(0) % parts * block
    tri = jnp.where(rows >= lax.broadcasted_iota(jnp.int32, (block, GROUP), 1), 1.0, 0.0).astype(BF16)
    spread = head_spread(heads)
    second = (pl.program_id(0) >= parts).astype(F32)
    core = (where_ref[3] == 1).astype(F32)
    mine, other = mine_ref[...].astype(F32), other_ref[...].astype(F32)
    chip = jnp.concatenate([(1.0 - core) * mine + core * other, (1.0 - core) * other + core * mine], 0)
    through = twin_ref[0:STATE, :].astype(F32) + factor_of(twin_ref, STATE) * chip
    arriving = ((1.0 - core) * chip + core * through).astype(BF16).astype(F32)
    carried = (1.0 - second + second * dec_ref[0:1, :]) * arriving + second * local_ref[...]
    crossed = contract(read_ref[...], carried.astype(BF16), 1, 0)
    fresh = 1.0 - start_ref[:, 0:1].astype(F32)
    reach = spread_wide(jnp.exp(sums_by_column(log_ref[...], tri)) * fresh, spread)
    gate = gate_ref[...].astype(F32)
    g = (direct_ref[...] + crossed * reach) * (gate / (1.0 + jnp.exp(-gate)))
    out_ref[...] = (g * gain_ref[...]).astype(BF16)
    squares = jnp.broadcast_to(jnp.sum(g * g, axis=1, keepdims=True), (block, 128))
    sq_ref[...] = jnp.transpose(squares)[0:8, :]


def assemble_kernel(where_ref, g_ref, *refs):
    own_ref, twin_ref, out_ref, w_ref = refs
    x_size, z_size, cores, rows, _ = w_ref.shape
    head, x_at, z_at, core = (where_ref[i] for i in range(4))

    def place(ref, base, x, k):
        way = jnp.where(k == 0, z_size - 1, 1)
        slots = [(z_at, k)]
        for turn in range(1, z_size // 2):
            z = (z_at + turn * way) % z_size
            slots += [(z, k), (z, 1 - k)]
        slots.append(((z_at + z_size // 2) % z_size, k))
        for slot, (z, block) in enumerate(slots):
            w_ref[x % x_size, z, block] = ref[base + slot]

    def one_x(turn, _):
        by = jnp.where(turn == 0, 0, jnp.where(turn == 1, x_size - 1, turn - 1))
        place(own_ref, turn * z_size, x_at + by, core)
        place(twin_ref, turn * z_size, x_at + by, 1 - core)

    lax.fori_loop(0, x_size, one_x, None)
    width = out_ref.shape[1]
    at = pl.multiple_of(((head + 2) % 4) * width, width)
    weights = w_ref[:, :, :, :, pl.ds(at, width)].reshape(g_ref.shape[1], width)
    out_ref[...] = contract(g_ref[...], weights, 1, 0).astype(BF16)


def product_kernel(head_ref, a_ref, w_ref, out_ref):
    weights = w_ref[...].reshape(a_ref.shape[1], w_ref.shape[-1])
    out_ref[0] = contract(a_ref[...], weights, 1, 0)


def down_kernel(where_ref, a_ref, w_ref, out_ref):
    block = a_ref.shape[1] // 4
    total = 0.0
    for x in range(4):
        weights = w_ref[:, (x - where_ref[1]) % 4].reshape(block, w_ref.shape[-1])
        total = total + contract(a_ref[:, x * block : (x + 1) * block], weights, 1, 0)
    out_ref[0] = total


def gained(ref, gain_ref, head, by):
    width = ref.shape[1]
    at = pl.multiple_of(((head + by) % 4) * width, width)
    return (ref[...].astype(F32) * gain_ref[:, pl.ds(at, width)]).astype(BF16)


def row_squares(ref):
    v = ref[...].astype(F32)
    return jnp.broadcast_to(jnp.sum(v * v, axis=1, keepdims=True), (ref.shape[0], 128))


def flat(ref):
    return ref[...].reshape(ref.shape[0] * ref.shape[1] * ref.shape[2], ref.shape[3])


def near_kernel(head_ref, own_ref, prev_ref, next_ref, gain_ref, w_own_ref, w_prev_ref, w_next_ref, acc_ref, sq_ref, x_ref):
    @pl.when(pl.program_id(0) == 0)
    def _():
        total = 0.0
        for slot, (ref, by) in enumerate([(own_ref, 0), (prev_ref, 3), (next_ref, 1)]):
            x_ref[slot] = gained(ref, gain_ref, head_ref[0], by)
            total = total + row_squares(ref)
        sq_ref[...] = total

    acc_ref[...] = sum(contract(x_ref[i], flat(ref), 1, 0) for i, ref in enumerate([w_own_ref, w_prev_ref, w_next_ref]))


def act_kernel(
    head_ref, far_ref, gain_ref, w_gate_ref, w_up_ref, acc_ref, sq_ref, down_ref, act_ref, out_ref, x_ref, scale_ref, sum_ref
):
    step = pl.program_id(0)

    @pl.when(step == 0)
    def _():
        x_ref[...] = gained(far_ref, gain_ref, head_ref[0], 2)
        total = sq_ref[...] + row_squares(far_ref)
        scale_ref[...] = lax.rsqrt(total / (4 * far_ref.shape[1]) + EPS)
        sum_ref[...] = jnp.zeros_like(sum_ref)

    scale = scale_ref[:, 0:1]
    block = w_up_ref.shape[-1]
    gate = (acc_ref[:, :block] + contract(x_ref[...], flat(w_gate_ref), 1, 0)) * scale
    up = (acc_ref[:, block:] + contract(x_ref[...], flat(w_up_ref), 1, 0)) * scale
    act = (gate / (1.0 + jnp.exp(-gate)) * up).astype(BF16)
    act_ref[...] = act
    sum_ref[...] += contract(act, flat(down_ref), 1, 0)

    @pl.when(step == pl.num_programs(0) - 1)
    def _():
        out_ref[...] = sum_ref[...].astype(BF16)


def along_x(array, by, x_size, z_size):
    row = 2 * z_size
    return lax.ppermute(array, "ctx", [(i, (i + by * row) % (x_size * row)) for i in range(x_size * row)])


def moved(array, axis, x_size, z_size, far=1):
    pairs = []
    for x in range(x_size):
        for z in range(z_size):
            for core in range(2):
                by = far * (1 - 2 * core)
                to = {
                    "x": ((x + by) % x_size, z, core),
                    "z": (x, (z + by) % z_size, core),
                    "core": (x, z, 1 - core),
                }[axis]
                pairs.append(((x * z_size + z) * 2 + core, (to[0] * z_size + to[1]) * 2 + to[2]))
    return lax.ppermute(array, "ctx", pairs)


def sent(array, by):
    return lax.ppermute(array, "head", [(i, (i + by) % 4) for i in range(4)])


def scattered(far, parts):
    half = far.shape[0] // 2
    first, second = sent(far[:half], 1), sent(far[half:], -1)
    one, three, own = parts()
    one = jnp.concatenate([one[:half] + first.astype(F32), one[half:]], 0).astype(BF16)
    three = jnp.concatenate([three[:half], three[half:] + second.astype(F32)], 0).astype(BF16)
    return own + sent(one, 1).astype(F32) + sent(three, -1).astype(F32)


def shards(
    mixer_input,
    gate_input,
    write_vecs,
    read_vecs,
    log_decay,
    doc_start,
    live_mask,
    skip_gain,
    norm_gain,
    residual,
    out_weight,
    mlp_gain,
    gate_weight,
    up_weight,
    down_weight,
):
    tokens, inner = mixer_input.shape
    heads = log_decay.shape[0]
    peers = lax.axis_size("ctx")
    width = residual.shape[1]
    model = out_weight.shape[1]
    units = gate_weight.shape[1]
    in_rows, ff_rows, out_rows = gate_weight.shape[0], down_weight.shape[0], out_weight.shape[0]
    x_size = 4
    z_size = peers // (2 * x_size)

    packed = jnp.concatenate([jnp.concatenate([gate_weight, up_weight], 1), down_weight], 0)

    in_hbm = lambda a: pltpu.with_memory_space_constraint(a, pltpu.HBM)
    mixer_input, gate_input, write_vecs, read_vecs, log_decay = map(
        in_hbm, (mixer_input, gate_input, write_vecs, read_vecs, log_decay)
    )
    starts = doc_start.reshape(1, tokens)
    live = live_mask.reshape(1, tokens)
    skip = jnp.repeat(skip_gain, HDIM).reshape(1, inner)
    gain = norm_gain.reshape(1, inner)
    at = lax.axis_index("ctx")
    where = jnp.stack([lax.axis_index("head"), at // (2 * z_size), at // 2 % z_size, at % 2])

    entire = lambda shape: pl.BlockSpec(shape, lambda i: (0,) * len(shape))
    state_in = (mixer_input, write_vecs, log_decay, starts, live)
    state_out = (((STATE + 16, inner), BF16), ((STATE, inner), F32), ((8, inner), F32))
    payload, local_0, dec_0 = pl.pallas_call(
        state_kernel,
        grid=(1,),
        out_shape=tuple(jax.ShapeDtypeStruct(*o) for o in state_out),
        in_specs=[entire(a.shape) for a in state_in],
        out_specs=tuple(entire(o[0]) for o in state_out),
        compiler_params=params(),
        name="state",
    )(*state_in)

    def passed(array, by):
        return lax.ppermute(array, "ctx", [(i, i + by) for i in range(peers - by)])

    def joined(kernel, name, *arrays):
        return pl.pallas_call(
            kernel,
            out_shape=jax.ShapeDtypeStruct((STATE // 2 + 16, inner), BF16),
            in_specs=[pl.BlockSpec(memory_space=pltpu.SMEM if a.ndim == 1 else pltpu.VMEM) for a in arrays],
            out_specs=vmem(),
            compiler_params=params(),
            name=name,
        )(*arrays)

    by_group = pl.BlockSpec((GROUP, inner), lambda g: (g, 0))
    vecs = pl.BlockSpec((GROUP, STATE), lambda g: (g, 0))
    logs = pl.BlockSpec((heads, GROUP), lambda g: (0, g))
    flags = pl.BlockSpec((1, GROUP), lambda g: (0, g))
    whole = lambda a: pl.BlockSpec(a.shape, lambda g: (0,) * a.ndim)
    some = heads // 2
    direct = pl.pallas_call(
        intra_kernel,
        grid=(tokens // GROUP, 2),
        out_shape=jax.ShapeDtypeStruct((tokens, inner), F32),
        in_specs=[
            pl.BlockSpec((GROUP, inner // 2), lambda g, k: (g, k)),
            pl.BlockSpec((GROUP, STATE), lambda g, k: (g, 0)),
            pl.BlockSpec((GROUP, STATE), lambda g, k: (g, 0)),
            pl.BlockSpec((some, GROUP), lambda g, k: (k, g)),
            pl.BlockSpec((1, GROUP), lambda g, k: (0, g)),
            pl.BlockSpec((1, inner // 2), lambda g, k: (0, k)),
        ],
        out_specs=pl.BlockSpec((GROUP, inner // 2), lambda g, k: (g, k)),
        compiler_params=params(),
        name="intra",
    )(mixer_input, write_vecs, read_vecs, log_decay, live, skip)

    step = lambda array, axis, far=1: moved(array, axis, x_size, z_size, far)
    tie = lambda *arrays: lax.optimization_barrier(arrays)
    block = out_weight[None]
    row = lambda array, by: along_x(array, by, x_size, z_size)
    other, packed = tie(step(block, "core"), packed)
    beyond = row(packed, -1), step(packed, "x", 2), row(packed, 1)
    piece = jnp.concatenate([block, other], 0)
    reach = z_size // 2
    first, *pieces = [step(piece, "z", far) for far in range(1, reach)] + [step(piece[:1], "z", reach)]
    twin = step(payload, "core")
    chips = joined(pair_kernel, "pair", where, payload, twin)
    got = passed(chips, 2)
    first, *pieces, next_x, over_x, last_x, got = tie(first, *pieces, *beyond, got)
    around_z = [list(range(x * 2 * z_size, (x + 1) * 2 * z_size)) for x in range(x_size)]
    weights = lax.all_gather(jnp.stack([packed, next_x, over_x, last_x]), "ctx", axis=0, axis_index_groups=around_z)
    chips, first = tie(joined(join_kernel, "join", chips, got), first)
    column_parts = [block, first, *pieces]
    column = pl.pallas_call(
        stack_kernel,
        out_shape=jax.ShapeDtypeStruct((z_size, out_rows, model), BF16),
        in_specs=[vmem()] * len(column_parts),
        out_specs=vmem(),
        compiler_params=params(),
        name="column",
    )(*column_parts)
    got, behind, ahead, direct = tie(passed(chips, 4), row(column, 1), row(column, -1), direct)
    chips, behind, ahead = tie(joined(join_kernel, "join", chips, got), behind, ahead)
    reached = passed(chips[: STATE // 2], 2)
    ends = row(behind[:reach], 1), row(ahead[reach:], -1)
    *ends, reached = tie(*ends, reached)
    own_out = jnp.concatenate([column, behind, ahead, *ends], 0)
    twin_out = step(own_out, "core")
    reached_twin = step(reached, "core")

    part = GROUP // 2
    by_part = pl.BlockSpec((part, inner), lambda i: (i, 0))
    gated, squares = pl.pallas_call(
        gate_kernel,
        grid=(tokens // part,),
        out_shape=(
            jax.ShapeDtypeStruct((tokens, inner), BF16),
            jax.ShapeDtypeStruct((8, tokens), F32),
        ),
        in_specs=[
            pl.BlockSpec(memory_space=pltpu.SMEM),
            by_part,
            whole(reached),
            whole(reached_twin),
            whole(twin),
            whole(local_0),
            whole(dec_0),
            pl.BlockSpec((part, STATE), lambda i: (i, 0)),
            pl.BlockSpec((heads, GROUP), lambda i: (0, i * part // GROUP)),
            pl.BlockSpec((1, GROUP), lambda i: (0, i * part // GROUP)),
            by_part,
            whole(gain),
        ],
        out_specs=(by_part, pl.BlockSpec((8, part), lambda i: (0, i))),
        compiler_params=params(),
        name="gating",
    )(where, direct, reached, reached_twin, twin, local_0, dec_0, read_vecs, log_decay, starts, gate_input, gain)
    mine = squares[0]
    pair = mine + sent(mine, 2)
    total = pair + sent(pair, 1)
    row_scale = lax.rsqrt(total / INNER + EPS)

    def call(kernel, grid, ins, outs, scratch, name, *args):
        return pl.pallas_call(
            kernel,
            grid_spec=pltpu.PrefetchScalarGridSpec(
                num_scalar_prefetch=1,
                grid=grid,
                in_specs=[spec for spec, _ in ins],
                out_specs=[spec for spec, _ in outs],
                scratch_shapes=scratch,
            ),
            out_shape=[shape for _, shape in outs],
            compiler_params=params(),
            name=name,
        )(*args, *[array for _, array in ins])

    def fixed(array):
        return pl.BlockSpec(array.shape, lambda j, h: (0,) * array.ndim), array

    def new(shape, dtype, block=None, index=None):
        index = index or (lambda j, h: (0,) * len(shape))
        return pl.BlockSpec(block or shape, index), jax.ShapeDtypeStruct(shape, dtype)

    share = (tokens, width)
    grid_of_rows = (x_size, z_size, 2, out_rows, model)
    far, rows_in_order = call(
        assemble_kernel,
        (1,),
        [fixed(a) for a in (gated, own_out, twin_out)],
        [new(share, BF16), new(grid_of_rows, BF16)],
        [],
        "assemble",
        where,
    )

    def others(kernel, array, spec, name):
        (parts,) = call(
            kernel,
            (3,),
            [fixed(array), spec],
            [new((3, *share), F32, (1, *share), lambda j, h: (j, 0, 0))],
            [],
            name,
            where,
        )
        return parts[0], parts[1], parts[2]

    part_of = lambda j, h: (h[0] + jnp.where(j == 2, 0, 2 * j + 1)) % 4
    by_column = pl.BlockSpec((*grid_of_rows[:4], width), lambda j, h: (0, 0, 0, 0, part_of(j, h)))
    summed = scattered(far, lambda: others(product_kernel, gated, (by_column, rows_in_order), "project"))
    hidden = (residual.astype(F32) + summed * row_scale[:, None]).astype(BF16)

    half = tokens // 2
    mlp_gains = mlp_gain.reshape(1, model)
    blocks = 2 * z_size

    def rows_of(by, block, index):
        return pl.BlockSpec((blocks, 1, in_rows, block), lambda j, h: (0, (h[0] + by - h[1]) % 4, 0, index(j))), weights

    wide = (tokens, 2 * units)
    hidden, weights = tie(hidden, weights)
    weights = in_hbm(weights)
    prev, following = sent(hidden, 1), sent(hidden, -1)
    prev, following = tie(prev, following)
    ends = sent(prev[:half], 1), sent(following[half:], -1)
    ff_block = 256
    ff_steps = units // ff_block
    paired = lambda j: j % 2 * ff_steps + j // 2
    acc, squares = call(
        near_kernel,
        (2 * ff_steps,),
        [
            fixed(hidden),
            fixed(prev),
            fixed(following),
            fixed(mlp_gains),
            rows_of(0, ff_block, paired),
            rows_of(3, ff_block, paired),
            rows_of(1, ff_block, paired),
        ],
        [new(wide, F32, (tokens, ff_block), lambda j, h: (0, j)), new((tokens, 128), F32)],
        [pltpu.VMEM((3, *share), BF16)],
        "mlp_near",
        where,
    )
    down_spec = pl.BlockSpec(
        (blocks, 1, ff_rows, width), lambda j, h: (0, (j - h[1]) % 4, in_rows // ff_rows, (h[0] + 2) % 4)
    )
    act, far = call(
        act_kernel,
        (ff_steps,),
        [
            fixed(jnp.concatenate(ends, 0)),
            fixed(mlp_gains),
            rows_of(2, ff_block, lambda j: j),
            rows_of(2, ff_block, lambda j: ff_steps + j),
            (pl.BlockSpec((tokens, 2 * ff_block), lambda j, h: (0, j)), acc),
            fixed(squares),
            (down_spec, weights),
        ],
        [new((tokens, units), BF16, (tokens, ff_block), lambda j, h: (0, j)), new(share, BF16)],
        [pltpu.VMEM(share, BF16), pltpu.VMEM((tokens, 128), F32), pltpu.VMEM(share, F32)],
        "mlp_act",
        where,
    )
    by_column = pl.BlockSpec(
        (blocks, x_size, ff_rows, width),
        lambda j, h: (0, 0, in_rows // ff_rows, part_of(j, h)),
    )
    added = scattered(far, lambda: others(down_kernel, act, (by_column, weights), "mlp_down"))
    return (live_mask.astype(F32)[:, None] * (hidden.astype(F32) + added)).astype(BF16)


def solution(mesh):
    return jax.shard_map(
        shards,
        mesh=mesh,
        in_specs=(
            P("ctx", "head"),
            P("ctx", "head"),
            P("ctx", None),
            P("ctx", None),
            P("head", "ctx"),
            P("ctx"),
            P("ctx"),
            P("head"),
            P("head"),
            P("ctx", "head"),
            P(("head", "ctx"), None),
            P(),
            P("ctx", "head"),
            P("ctx", "head"),
            P(("head", "ctx"), None),
        ),
        out_specs=P("ctx", "head"),
        check_vma=False,
    )
```

```python
import jax
import jax.numpy as jnp
from jax import lax
from jax.experimental import pallas as pl
from jax.experimental.pallas import tpu as pltpu
from jax.sharding import PartitionSpec as P

HDIM = 64
STATE = 128
GROUP = 256
DOC_GROUPS = 16
INNER = 4096
EPS = 1e-05
F32 = jnp.float32
BF16 = jnp.bfloat16


def params(mib=28):
    return pltpu.CompilerParams(vmem_limit_bytes=mib * 1024 * 1024)


def vmem():
    return pl.BlockSpec(memory_space=pltpu.VMEM)


def contract(a, b, da, db):
    return lax.dot_general(a, b, (((da,), (db,)), ((), ())), preferred_element_type=F32)


def split2(v):
    hi = v.astype(BF16)
    return hi, (v - hi.astype(F32)).astype(BF16)


def split3(v):
    hi = v.astype(BF16)
    rest = v - hi.astype(F32)
    mid = rest.astype(BF16)
    return hi, mid, (rest - mid.astype(F32)).astype(BF16)


def tri_ones(n):
    rows = lax.broadcasted_iota(jnp.int32, (n, n), 0)
    cols = lax.broadcasted_iota(jnp.int32, (n, n), 1)
    return jnp.where(rows >= cols, 1.0, 0.0).astype(BF16), jnp.where(rows == cols, 1.0, 0.0).astype(BF16)


def head_spread(heads):
    rows = lax.broadcasted_iota(jnp.int32, (heads, heads * HDIM), 0)
    cols = lax.broadcasted_iota(jnp.int32, (heads, heads * HDIM), 1)
    return jnp.where(cols // HDIM == rows, 1.0, 0.0).astype(BF16)


def spread_wide(cols, spread):
    hi, lo = split2(cols)
    return contract(hi, spread, 1, 0) + contract(lo, spread, 1, 0)


def sums_by_row(log_group, tri):
    return sum(contract(part, tri, 1, 1) for part in split3(log_group))


def sums_by_column(log_group, tri):
    return sum(contract(tri, part, 1, 1) for part in split3(log_group))


def column_of(row, eye):
    return contract(eye, jnp.broadcast_to(row.astype(F32), (16, row.shape[1])).astype(BF16), 1, 1)


def state_kernel(x_ref, write_ref, log_ref, start_ref, live_ref, pay_ref, local_ref, dec_ref):
    heads = log_ref.shape[0]
    tri, eye = tri_ones(GROUP)
    spread = head_spread(heads)
    locals_, decays = [], []
    for g in range(2):
        rows = slice(g * GROUP, (g + 1) * GROUP)
        sums = sums_by_column(log_ref[:, rows], tri)
        last = sums[GROUP - 1 : GROUP, :]
        live = column_of(live_ref[:, rows], eye)
        tail = spread_wide(jnp.exp(last - sums) * live, spread)
        scaled = (x_ref[rows, :].astype(F32) * tail).astype(BF16)
        locals_.append(contract(write_ref[rows, :], scaled, 0, 0))
        fresh = 1.0 - start_ref[:, g * GROUP : g * GROUP + 1].astype(F32)
        end = jnp.broadcast_to(jnp.exp(last) * fresh, (16, heads))
        decays.append(sum(contract(part, spread, 1, 0) for part in split3(end)))
    state = decays[1][0:1] * locals_[0] + locals_[1]
    pay_ref[0:STATE, :] = state.astype(BF16)
    pay_ref[STATE : STATE + 16, :] = factor_rows((decays[0] * decays[1])[0:1])
    local_ref[...] = locals_[0]
    dec_ref[...] = decays[0][0:8]


def stack_kernel(*refs):
    at = 0
    for ref in refs[:-1]:
        refs[-1][at : at + ref.shape[0]] = ref[...]
        at += ref.shape[0]


def factor_of(ref, at):
    tail = ref[at : at + 16, :].astype(F32)
    return tail[0:1] + tail[1:2] + tail[2:3]


def factor_rows(factor):
    both = jnp.broadcast_to(factor, (16, factor.shape[1]))
    hi, mid, low = split3(both)
    row = lax.broadcasted_iota(jnp.int32, both.shape, 0)
    packed = jnp.where(row == 0, hi.astype(F32), jnp.where(row == 1, mid.astype(F32), low.astype(F32)))
    return packed.astype(BF16)


def pair_kernel(where_ref, mine_ref, twin_ref, out_ref):
    core = where_ref[3]
    half = STATE // 2
    at = pl.multiple_of(core * half, half)
    mine, twin = factor_of(mine_ref, STATE), factor_of(twin_ref, STATE)
    own = mine_ref[pl.ds(at, half), :].astype(F32)
    got = twin_ref[pl.ds(at, half), :].astype(F32)
    second = (core == 1).astype(F32)
    state = second * (own + mine * got) + (1.0 - second) * (got + twin * own)
    out_ref[0:half, :] = state.astype(BF16)
    out_ref[half : half + 16, :] = factor_rows(mine * twin)


def join_kernel(own_ref, got_ref, out_ref):
    half = STATE // 2
    mine = factor_of(own_ref, half)
    state = own_ref[0:half, :].astype(F32) + mine * got_ref[0:half, :].astype(F32)
    out_ref[0:half, :] = state.astype(BF16)
    out_ref[half : half + 16, :] = factor_rows(mine * factor_of(got_ref, half))


def intra_kernel(x_ref, write_ref, read_ref, log_ref, live_ref, skip_ref, out_ref):
    heads = log_ref.shape[0]
    tri, eye = tri_ones(GROUP)
    half = GROUP // 2
    live = column_of(live_ref[...], eye)[:, 0:1].astype(BF16)
    by_row = sums_by_row(log_ref[...], tri)
    by_col = sums_by_column(log_ref[...], tri)
    scores = contract(read_ref[...], write_ref[...], 1, 1)
    scores = jnp.where(tri > 0, scores, 0.0)
    lane = lax.broadcasted_iota(jnp.int32, (GROUP, 2 * HDIM), 1)
    for pair in range(heads // 2):
        cols = slice(pair * 2 * HDIM, (pair + 1) * 2 * HDIM)
        x = x_ref[:, cols] * live
        top = bottom = 0.0
        for k in range(2):
            h = 2 * pair + k
            mine = jnp.where((lane < HDIM) == (k == 0), x, jnp.zeros_like(x))
            row = by_row[h : h + 1, :]
            col = by_col[:, h : h + 1]
            gap = jnp.minimum(col[:half] - row[:, :half], 0.0)
            w = (scores[:half, :half] * jnp.exp(gap)).astype(BF16)
            top = top + contract(w, mine[:half], 1, 0)
            gap = jnp.minimum(col[half:] - row, 0.0)
            w = (scores[half:] * jnp.exp(gap)).astype(BF16)
            bottom = bottom + contract(w, mine, 1, 0)
        direct = skip_ref[:, cols] * x.astype(F32)
        out_ref[:half, cols] = top + direct[:half]
        out_ref[half:, cols] = bottom + direct[half:]


def gate_kernel(where_ref, direct_ref, mine_ref, other_ref, twin_ref, local_ref, dec_ref, read_ref, log_ref, start_ref, gate_ref, gain_ref, out_ref, sq_ref):
    heads = log_ref.shape[0]
    block = out_ref.shape[0]
    parts = GROUP // block
    rows = lax.broadcasted_iota(jnp.int32, (block, GROUP), 0) + pl.program_id(0) % parts * block
    tri = jnp.where(rows >= lax.broadcasted_iota(jnp.int32, (block, GROUP), 1), 1.0, 0.0).astype(BF16)
    spread = head_spread(heads)
    second = (pl.program_id(0) >= parts).astype(F32)
    core = (where_ref[3] == 1).astype(F32)
    mine, other = mine_ref[...].astype(F32), other_ref[...].astype(F32)
    chip = jnp.concatenate([(1.0 - core) * mine + core * other, (1.0 - core) * other + core * mine], 0)
    through = twin_ref[0:STATE, :].astype(F32) + factor_of(twin_ref, STATE) * chip
    arriving = ((1.0 - core) * chip + core * through).astype(BF16).astype(F32)
    carried = (1.0 - second + second * dec_ref[0:1, :]) * arriving + second * local_ref[...]
    crossed = contract(read_ref[...], carried.astype(BF16), 1, 0)
    fresh = 1.0 - start_ref[:, 0:1].astype(F32)
    reach = spread_wide(jnp.exp(sums_by_column(log_ref[...], tri)) * fresh, spread)
    gate = gate_ref[...].astype(F32)
    g = (direct_ref[...] + crossed * reach) * (gate / (1.0 + jnp.exp(-gate)))
    out_ref[...] = (g * gain_ref[...]).astype(BF16)
    squares = jnp.broadcast_to(jnp.sum(g * g, axis=1, keepdims=True), (block, 128))
    sq_ref[...] = jnp.transpose(squares)[0:8, :]


def assemble_kernel(where_ref, g_ref, *refs):
    own_ref, twin_ref, out_ref, w_ref = refs
    x_size, z_size, cores, rows, _ = w_ref.shape
    head, x_at, z_at, core = (where_ref[i] for i in range(4))

    def place(ref, base, x, k):
        way = jnp.where(k == 0, z_size - 1, 1)
        slots = [(z_at, k)]
        for turn in range(1, z_size // 2):
            z = (z_at + turn * way) % z_size
            slots += [(z, k), (z, 1 - k)]
        slots.append(((z_at + z_size // 2) % z_size, k))
        for slot, (z, block) in enumerate(slots):
            w_ref[x % x_size, z, block] = ref[base + slot]

    def one_x(turn, _):
        by = jnp.where(turn == 0, 0, jnp.where(turn == 1, x_size - 1, turn - 1))
        place(own_ref, turn * z_size, x_at + by, core)
        place(twin_ref, turn * z_size, x_at + by, 1 - core)

    lax.fori_loop(0, x_size, one_x, None)
    width = out_ref.shape[1]
    at = pl.multiple_of(((head + 2) % 4) * width, width)
    weights = w_ref[:, :, :, :, pl.ds(at, width)].reshape(g_ref.shape[1], width)
    out_ref[...] = contract(g_ref[...], weights, 1, 0).astype(BF16)


def product_kernel(head_ref, a_ref, w_ref, out_ref):
    weights = w_ref[...].reshape(a_ref.shape[1], w_ref.shape[-1])
    out_ref[0] = contract(a_ref[...], weights, 1, 0)


def down_kernel(where_ref, a_ref, w_ref, out_ref):
    block = a_ref.shape[1] // 4
    total = 0.0
    for x in range(4):
        weights = w_ref[:, (x - where_ref[1]) % 4].reshape(block, w_ref.shape[-1])
        total = total + contract(a_ref[:, x * block : (x + 1) * block], weights, 1, 0)
    out_ref[0] = total


def gained(ref, gain_ref, head, by):
    width = ref.shape[1]
    at = pl.multiple_of(((head + by) % 4) * width, width)
    return (ref[...].astype(F32) * gain_ref[:, pl.ds(at, width)]).astype(BF16)


def row_squares(ref):
    v = ref[...].astype(F32)
    return jnp.broadcast_to(jnp.sum(v * v, axis=1, keepdims=True), (ref.shape[0], 128))


def flat(ref):
    return ref[...].reshape(ref.shape[0] * ref.shape[1] * ref.shape[2], ref.shape[3])


def near_kernel(head_ref, own_ref, prev_ref, next_ref, gain_ref, w_ref, acc_ref, sq_ref, x_ref):
    step = pl.program_id(0)

    @pl.when(step == 0)
    def _():
        total = 0.0
        for slot, (ref, by) in enumerate([(own_ref, 0), (prev_ref, 3), (next_ref, 1)]):
            x_ref[slot] = gained(ref, gain_ref, head_ref[0], by)
            total = total + row_squares(ref)
        sq_ref[...] = total

    block = 256
    pairs = acc_ref.shape[1] // block // 2
    rows = w_ref.shape[0] * w_ref.shape[2]

    def columns(n, _):
        at = pl.multiple_of(n * block, block)
        of = pl.multiple_of((n % 2 * pairs + n // 2) * block, block)
        part = contract(x_ref[step], w_ref[:, 0, :, pl.ds(of, block)].reshape(rows, block), 1, 0)
        acc_ref[:, pl.ds(at, block)] = jnp.where(step == 0, part, acc_ref[:, pl.ds(at, block)] + part)

    lax.fori_loop(0, 2 * pairs, columns, None)


def act_kernel(
    head_ref, far_ref, gain_ref, w_gate_ref, w_up_ref, acc_ref, sq_ref, down_ref, act_ref, out_ref, x_ref, scale_ref, sum_ref
):
    step = pl.program_id(0)

    @pl.when(step == 0)
    def _():
        x_ref[...] = gained(far_ref, gain_ref, head_ref[0], 2)
        total = sq_ref[...] + row_squares(far_ref)
        scale_ref[...] = lax.rsqrt(total / (4 * far_ref.shape[1]) + EPS)
        sum_ref[...] = jnp.zeros_like(sum_ref)

    scale = scale_ref[:, 0:1]
    block = w_up_ref.shape[-1]
    gate = (acc_ref[:, :block] + contract(x_ref[...], flat(w_gate_ref), 1, 0)) * scale
    up = (acc_ref[:, block:] + contract(x_ref[...], flat(w_up_ref), 1, 0)) * scale
    act = (gate / (1.0 + jnp.exp(-gate)) * up).astype(BF16)
    act_ref[...] = act
    sum_ref[...] += contract(act, flat(down_ref), 1, 0)

    @pl.when(step == pl.num_programs(0) - 1)
    def _():
        out_ref[...] = sum_ref[...].astype(BF16)


def along_x(array, by, x_size, z_size):
    row = 2 * z_size
    return lax.ppermute(array, "ctx", [(i, (i + by * row) % (x_size * row)) for i in range(x_size * row)])


def moved(array, axis, x_size, z_size, far=1):
    pairs = []
    for x in range(x_size):
        for z in range(z_size):
            for core in range(2):
                by = far * (1 - 2 * core)
                to = {
                    "x": ((x + by) % x_size, z, core),
                    "z": (x, (z + by) % z_size, core),
                    "core": (x, z, 1 - core),
                }[axis]
                pairs.append(((x * z_size + z) * 2 + core, (to[0] * z_size + to[1]) * 2 + to[2]))
    return lax.ppermute(array, "ctx", pairs)


def sent(array, by):
    return lax.ppermute(array, "head", [(i, (i + by) % 4) for i in range(4)])


def scattered(far, parts, beside=None):
    half = far.shape[0] // 2
    first, second = sent(far[:half], 1), sent(far[half:], -1)
    if beside is not None:
        first, second, beside = lax.optimization_barrier((first, second, beside))
    one, three, own = parts()
    one = jnp.concatenate([one[:half] + first.astype(F32), one[half:]], 0).astype(BF16)
    three = jnp.concatenate([three[:half], three[half:] + second.astype(F32)], 0).astype(BF16)
    return own + sent(one, 1).astype(F32) + sent(three, -1).astype(F32), beside


def shards(
    mixer_input,
    gate_input,
    write_vecs,
    read_vecs,
    log_decay,
    doc_start,
    live_mask,
    skip_gain,
    norm_gain,
    residual,
    out_weight,
    mlp_gain,
    gate_weight,
    up_weight,
    down_weight,
):
    tokens, inner = mixer_input.shape
    heads = log_decay.shape[0]
    peers = lax.axis_size("ctx")
    width = residual.shape[1]
    model = out_weight.shape[1]
    units = gate_weight.shape[1]
    in_rows, ff_rows, out_rows = gate_weight.shape[0], down_weight.shape[0], out_weight.shape[0]
    x_size = 4
    z_size = peers // (2 * x_size)

    packed = jnp.concatenate([jnp.concatenate([gate_weight, up_weight], 1), down_weight], 0)

    in_hbm = lambda a: pltpu.with_memory_space_constraint(a, pltpu.HBM)
    mixer_input, gate_input, write_vecs, read_vecs, log_decay = map(
        in_hbm, (mixer_input, gate_input, write_vecs, read_vecs, log_decay)
    )
    starts = doc_start.reshape(1, tokens)
    live = live_mask.reshape(1, tokens)
    skip = jnp.repeat(skip_gain, HDIM).reshape(1, inner)
    gain = norm_gain.reshape(1, inner)
    at = lax.axis_index("ctx")
    where = jnp.stack([lax.axis_index("head"), at // (2 * z_size), at // 2 % z_size, at % 2])

    entire = lambda shape: pl.BlockSpec(shape, lambda i: (0,) * len(shape))
    state_in = (mixer_input, write_vecs, log_decay, starts, live)
    state_out = (((STATE + 16, inner), BF16), ((STATE, inner), F32), ((8, inner), F32))
    payload, local_0, dec_0 = pl.pallas_call(
        state_kernel,
        grid=(1,),
        out_shape=tuple(jax.ShapeDtypeStruct(*o) for o in state_out),
        in_specs=[entire(a.shape) for a in state_in],
        out_specs=tuple(entire(o[0]) for o in state_out),
        compiler_params=params(),
        name="state",
    )(*state_in)

    def passed(array, by):
        return lax.ppermute(array, "ctx", [(i, i + by) for i in range(peers - by)])

    def joined(kernel, name, *arrays):
        return pl.pallas_call(
            kernel,
            out_shape=jax.ShapeDtypeStruct((STATE // 2 + 16, inner), BF16),
            in_specs=[pl.BlockSpec(memory_space=pltpu.SMEM if a.ndim == 1 else pltpu.VMEM) for a in arrays],
            out_specs=vmem(),
            compiler_params=params(),
            name=name,
        )(*arrays)

    by_group = pl.BlockSpec((GROUP, inner), lambda g: (g, 0))
    vecs = pl.BlockSpec((GROUP, STATE), lambda g: (g, 0))
    logs = pl.BlockSpec((heads, GROUP), lambda g: (0, g))
    flags = pl.BlockSpec((1, GROUP), lambda g: (0, g))
    whole = lambda a: pl.BlockSpec(a.shape, lambda g: (0,) * a.ndim)
    some = heads // 2
    direct = pl.pallas_call(
        intra_kernel,
        grid=(tokens // GROUP, 2),
        out_shape=jax.ShapeDtypeStruct((tokens, inner), F32),
        in_specs=[
            pl.BlockSpec((GROUP, inner // 2), lambda g, k: (g, k)),
            pl.BlockSpec((GROUP, STATE), lambda g, k: (g, 0)),
            pl.BlockSpec((GROUP, STATE), lambda g, k: (g, 0)),
            pl.BlockSpec((some, GROUP), lambda g, k: (k, g)),
            pl.BlockSpec((1, GROUP), lambda g, k: (0, g)),
            pl.BlockSpec((1, inner // 2), lambda g, k: (0, k)),
        ],
        out_specs=pl.BlockSpec((GROUP, inner // 2), lambda g, k: (g, k)),
        compiler_params=params(),
        name="intra",
    )(mixer_input, write_vecs, read_vecs, log_decay, live, skip)

    step = lambda array, axis, far=1: moved(array, axis, x_size, z_size, far)
    tie = lambda *arrays: lax.optimization_barrier(arrays)
    block = out_weight[None]
    row = lambda array, by: along_x(array, by, x_size, z_size)
    other, packed = tie(step(block, "core"), packed)
    beyond = row(packed, -1), step(packed, "x", 2), row(packed, 1)
    piece = jnp.concatenate([block, other], 0)
    reach = z_size // 2
    first, *pieces = [step(piece, "z", far) for far in range(1, reach)] + [step(piece[:1], "z", reach)]
    twin = step(payload, "core")
    chips = joined(pair_kernel, "pair", where, payload, twin)
    got = passed(chips, 2)
    first, *pieces, next_x, over_x, last_x, got = tie(first, *pieces, *beyond, got)
    around_z = [list(range(x * 2 * z_size, (x + 1) * 2 * z_size)) for x in range(x_size)]
    weights = lax.all_gather(jnp.stack([packed, next_x, over_x, last_x]), "ctx", axis=0, axis_index_groups=around_z)
    chips, first = tie(joined(join_kernel, "join", chips, got), first)
    column_parts = [block, first, *pieces]
    column = pl.pallas_call(
        stack_kernel,
        out_shape=jax.ShapeDtypeStruct((z_size, out_rows, model), BF16),
        in_specs=[vmem()] * len(column_parts),
        out_specs=vmem(),
        compiler_params=params(),
        name="column",
    )(*column_parts)
    got, behind, ahead, direct = tie(passed(chips, 4), row(column, 1), row(column, -1), direct)
    chips, behind, ahead = tie(joined(join_kernel, "join", chips, got), behind, ahead)
    reached = passed(chips[: STATE // 2], 2)
    ends = row(behind[:reach], 1), row(ahead[reach:], -1)
    *ends, reached = tie(*ends, reached)
    own_out = jnp.concatenate([column, behind, ahead, *ends], 0)
    twin_out = step(own_out, "core")
    reached_twin = step(reached, "core")

    part = GROUP // 2
    by_part = pl.BlockSpec((part, inner), lambda i: (i, 0))
    gated, squares = pl.pallas_call(
        gate_kernel,
        grid=(tokens // part,),
        out_shape=(
            jax.ShapeDtypeStruct((tokens, inner), BF16),
            jax.ShapeDtypeStruct((8, tokens), F32),
        ),
        in_specs=[
            pl.BlockSpec(memory_space=pltpu.SMEM),
            by_part,
            whole(reached),
            whole(reached_twin),
            whole(twin),
            whole(local_0),
            whole(dec_0),
            pl.BlockSpec((part, STATE), lambda i: (i, 0)),
            pl.BlockSpec((heads, GROUP), lambda i: (0, i * part // GROUP)),
            pl.BlockSpec((1, GROUP), lambda i: (0, i * part // GROUP)),
            by_part,
            whole(gain),
        ],
        out_specs=(by_part, pl.BlockSpec((8, part), lambda i: (0, i))),
        compiler_params=params(),
        name="gating",
    )(where, direct, reached, reached_twin, twin, local_0, dec_0, read_vecs, log_decay, starts, gate_input, gain)
    mine = squares[0]
    pair = mine + sent(mine, 2)

    def call(kernel, grid, ins, outs, scratch, name, *args):
        return pl.pallas_call(
            kernel,
            grid_spec=pltpu.PrefetchScalarGridSpec(
                num_scalar_prefetch=1,
                grid=grid,
                in_specs=[spec for spec, _ in ins],
                out_specs=[spec for spec, _ in outs],
                scratch_shapes=scratch,
            ),
            out_shape=[shape for _, shape in outs],
            compiler_params=params(),
            name=name,
        )(*args, *[array for _, array in ins])

    def fixed(array):
        return pl.BlockSpec(array.shape, lambda j, h: (0,) * array.ndim), array

    def new(shape, dtype, block=None, index=None):
        index = index or (lambda j, h: (0,) * len(shape))
        return pl.BlockSpec(block or shape, index), jax.ShapeDtypeStruct(shape, dtype)

    share = (tokens, width)
    grid_of_rows = (x_size, z_size, 2, out_rows, model)
    far, rows_in_order = call(
        assemble_kernel,
        (1,),
        [fixed(a) for a in (gated, own_out, twin_out)],
        [new(share, BF16), new(grid_of_rows, BF16)],
        [],
        "assemble",
        where,
    )

    def others(kernel, array, spec, name):
        (parts,) = call(
            kernel,
            (3,),
            [fixed(array), spec],
            [new((3, *share), F32, (1, *share), lambda j, h: (j, 0, 0))],
            [],
            name,
            where,
        )
        return parts[0], parts[1], parts[2]

    part_of = lambda j, h: (h[0] + jnp.where(j == 2, 0, 2 * j + 1)) % 4
    by_column = pl.BlockSpec((*grid_of_rows[:4], width), lambda j, h: (0, 0, 0, 0, part_of(j, h)))
    far, pair = tie(far, pair)
    total = pair + sent(pair, 1)
    summed, total = scattered(far, lambda: others(product_kernel, gated, (by_column, rows_in_order), "project"), total)
    row_scale = lax.rsqrt(total / INNER + EPS)
    hidden = (residual.astype(F32) + summed * row_scale[:, None]).astype(BF16)

    half = tokens // 2
    mlp_gains = mlp_gain.reshape(1, model)
    blocks = 2 * z_size

    def rows_of(by, block, index):
        return pl.BlockSpec((blocks, 1, in_rows, block), lambda j, h: (0, (h[0] + by - h[1]) % 4, 0, index(j))), weights

    wide = (tokens, 2 * units)
    prev, following = sent(hidden, 1), sent(hidden, -1)
    prev, following, weights = tie(prev, following, weights)
    weights = in_hbm(weights)
    ends = sent(prev[:half], 1), sent(following[half:], -1)
    ff_block = 256
    ff_steps = units // ff_block
    acc, squares = call(
        near_kernel,
        (3,),
        [
            fixed(hidden),
            fixed(prev),
            fixed(following),
            fixed(mlp_gains),
            (
                pl.BlockSpec(
                    (blocks, 1, in_rows, 2 * units),
                    lambda j, h: (0, (h[0] + jnp.where(j == 1, 3, j // 2) - h[1]) % 4, 0, 0),
                ),
                weights,
            ),
        ],
        [new(wide, F32), new((tokens, 128), F32)],
        [pltpu.VMEM((3, *share), BF16)],
        "mlp_near",
        where,
    )
    down_spec = pl.BlockSpec(
        (blocks, 1, ff_rows, width), lambda j, h: (0, (j - h[1]) % 4, in_rows // ff_rows, (h[0] + 2) % 4)
    )
    act, far = call(
        act_kernel,
        (ff_steps,),
        [
            fixed(jnp.concatenate(ends, 0)),
            fixed(mlp_gains),
            rows_of(2, ff_block, lambda j: j),
            rows_of(2, ff_block, lambda j: ff_steps + j),
            (pl.BlockSpec((tokens, 2 * ff_block), lambda j, h: (0, j)), acc),
            fixed(squares),
            (down_spec, weights),
        ],
        [new((tokens, units), BF16, (tokens, ff_block), lambda j, h: (0, j)), new(share, BF16)],
        [pltpu.VMEM(share, BF16), pltpu.VMEM((tokens, 128), F32), pltpu.VMEM(share, F32)],
        "mlp_act",
        where,
    )
    by_column = pl.BlockSpec(
        (blocks, x_size, ff_rows, width),
        lambda j, h: (0, 0, in_rows // ff_rows, part_of(j, h)),
    )
    added, _ = scattered(far, lambda: others(down_kernel, act, (by_column, weights), "mlp_down"))
    return (live_mask.astype(F32)[:, None] * (hidden.astype(F32) + added)).astype(BF16)


def solution(mesh):
    return jax.shard_map(
        shards,
        mesh=mesh,
        in_specs=(
            P("ctx", "head"),
            P("ctx", "head"),
            P("ctx", None),
            P("ctx", None),
            P("head", "ctx"),
            P("ctx"),
            P("ctx"),
            P("head"),
            P("head"),
            P("ctx", "head"),
            P(("head", "ctx"), None),
            P(),
            P("ctx", "head"),
            P("ctx", "head"),
            P(("head", "ctx"), None),
        ),
        out_specs=P("ctx", "head"),
        check_vma=False,
    )
```

```python
import jax
import jax.numpy as jnp
from jax import lax
from jax.experimental import pallas as pl
from jax.experimental.pallas import tpu as pltpu
from jax.sharding import PartitionSpec as P

HDIM = 64
STATE = 128
GROUP = 256
DOC_GROUPS = 16
INNER = 4096
EPS = 1e-05
F32 = jnp.float32
BF16 = jnp.bfloat16


def params(mib=28):
    return pltpu.CompilerParams(vmem_limit_bytes=mib * 1024 * 1024)


def vmem():
    return pl.BlockSpec(memory_space=pltpu.VMEM)


def contract(a, b, da, db):
    return lax.dot_general(a, b, (((da,), (db,)), ((), ())), preferred_element_type=F32)


def split2(v):
    hi = v.astype(BF16)
    return hi, (v - hi.astype(F32)).astype(BF16)


def split3(v):
    hi = v.astype(BF16)
    rest = v - hi.astype(F32)
    mid = rest.astype(BF16)
    return hi, mid, (rest - mid.astype(F32)).astype(BF16)


def tri_ones(n):
    rows = lax.broadcasted_iota(jnp.int32, (n, n), 0)
    cols = lax.broadcasted_iota(jnp.int32, (n, n), 1)
    return jnp.where(rows >= cols, 1.0, 0.0).astype(BF16), jnp.where(rows == cols, 1.0, 0.0).astype(BF16)


def head_spread(heads):
    rows = lax.broadcasted_iota(jnp.int32, (heads, heads * HDIM), 0)
    cols = lax.broadcasted_iota(jnp.int32, (heads, heads * HDIM), 1)
    return jnp.where(cols // HDIM == rows, 1.0, 0.0).astype(BF16)


def spread_wide(cols, spread):
    hi, lo = split2(cols)
    return contract(hi, spread, 1, 0) + contract(lo, spread, 1, 0)


def sums_by_row(log_group, tri):
    return sum(contract(part, tri, 1, 1) for part in split3(log_group))


def sums_by_column(log_group, tri):
    return sum(contract(tri, part, 1, 1) for part in split3(log_group))


def column_of(row, eye):
    return contract(eye, jnp.broadcast_to(row.astype(F32), (16, row.shape[1])).astype(BF16), 1, 1)


def state_kernel(x_ref, write_ref, log_ref, start_ref, live_ref, pay_ref, local_ref, dec_ref):
    heads = log_ref.shape[0]
    tri, eye = tri_ones(GROUP)
    spread = head_spread(heads)
    locals_, decays = [], []
    for g in range(2):
        rows = slice(g * GROUP, (g + 1) * GROUP)
        sums = sums_by_column(log_ref[:, rows], tri)
        last = sums[GROUP - 1 : GROUP, :]
        live = column_of(live_ref[:, rows], eye)
        tail = spread_wide(jnp.exp(last - sums) * live, spread)
        scaled = (x_ref[rows, :].astype(F32) * tail).astype(BF16)
        locals_.append(contract(write_ref[rows, :], scaled, 0, 0))
        fresh = 1.0 - start_ref[:, g * GROUP : g * GROUP + 1].astype(F32)
        end = jnp.broadcast_to(jnp.exp(last) * fresh, (16, heads))
        decays.append(sum(contract(part, spread, 1, 0) for part in split3(end)))
    state = decays[1][0:1] * locals_[0] + locals_[1]
    pay_ref[0:STATE, :] = state.astype(BF16)
    pay_ref[STATE : STATE + 16, :] = factor_rows((decays[0] * decays[1])[0:1])
    local_ref[...] = locals_[0]
    dec_ref[...] = decays[0][0:8]


def stack_kernel(*refs):
    at = 0
    for ref in refs[:-1]:
        refs[-1][at : at + ref.shape[0]] = ref[...]
        at += ref.shape[0]


def factor_of(ref, at):
    tail = ref[at : at + 16, :].astype(F32)
    return tail[0:1] + tail[1:2] + tail[2:3]


def factor_rows(factor):
    both = jnp.broadcast_to(factor, (16, factor.shape[1]))
    hi, mid, low = split3(both)
    row = lax.broadcasted_iota(jnp.int32, both.shape, 0)
    packed = jnp.where(row == 0, hi.astype(F32), jnp.where(row == 1, mid.astype(F32), low.astype(F32)))
    return packed.astype(BF16)


def pair_kernel(where_ref, mine_ref, twin_ref, out_ref):
    core = where_ref[3]
    half = STATE // 2
    at = pl.multiple_of(core * half, half)
    mine, twin = factor_of(mine_ref, STATE), factor_of(twin_ref, STATE)
    own = mine_ref[pl.ds(at, half), :].astype(F32)
    got = twin_ref[pl.ds(at, half), :].astype(F32)
    second = (core == 1).astype(F32)
    state = second * (own + mine * got) + (1.0 - second) * (got + twin * own)
    out_ref[0:half, :] = state.astype(BF16)
    out_ref[half : half + 16, :] = factor_rows(mine * twin)


def join_kernel(own_ref, got_ref, out_ref):
    half = STATE // 2
    mine = factor_of(own_ref, half)
    state = own_ref[0:half, :].astype(F32) + mine * got_ref[0:half, :].astype(F32)
    out_ref[0:half, :] = state.astype(BF16)
    out_ref[half : half + 16, :] = factor_rows(mine * factor_of(got_ref, half))


def intra_kernel(x_ref, write_ref, read_ref, log_ref, live_ref, skip_ref, out_ref):
    heads = log_ref.shape[0]
    tri, eye = tri_ones(GROUP)
    half = GROUP // 2
    live = column_of(live_ref[...], eye)[:, 0:1].astype(BF16)
    by_row = sums_by_row(log_ref[...], tri)
    by_col = sums_by_column(log_ref[...], tri)
    scores = contract(read_ref[...], write_ref[...], 1, 1)
    scores = jnp.where(tri > 0, scores, 0.0)
    lane = lax.broadcasted_iota(jnp.int32, (GROUP, 2 * HDIM), 1)
    for pair in range(heads // 2):
        cols = slice(pair * 2 * HDIM, (pair + 1) * 2 * HDIM)
        x = x_ref[:, cols] * live
        top = bottom = 0.0
        for k in range(2):
            h = 2 * pair + k
            mine = jnp.where((lane < HDIM) == (k == 0), x, jnp.zeros_like(x))
            row = by_row[h : h + 1, :]
            col = by_col[:, h : h + 1]
            gap = jnp.minimum(col[:half] - row[:, :half], 0.0)
            w = (scores[:half, :half] * jnp.exp(gap)).astype(BF16)
            top = top + contract(w, mine[:half], 1, 0)
            gap = jnp.minimum(col[half:] - row, 0.0)
            w = (scores[half:] * jnp.exp(gap)).astype(BF16)
            bottom = bottom + contract(w, mine, 1, 0)
        direct = skip_ref[:, cols] * x.astype(F32)
        out_ref[:half, cols] = top + direct[:half]
        out_ref[half:, cols] = bottom + direct[half:]


def gate_kernel(where_ref, direct_ref, mine_ref, other_ref, twin_ref, local_ref, dec_ref, read_ref, log_ref, start_ref, gate_ref, gain_ref, out_ref, sq_ref):
    heads = log_ref.shape[0]
    block = out_ref.shape[0]
    parts = GROUP // block
    rows = lax.broadcasted_iota(jnp.int32, (block, GROUP), 0) + pl.program_id(0) % parts * block
    tri = jnp.where(rows >= lax.broadcasted_iota(jnp.int32, (block, GROUP), 1), 1.0, 0.0).astype(BF16)
    spread = head_spread(heads)
    second = (pl.program_id(0) >= parts).astype(F32)
    core = (where_ref[3] == 1).astype(F32)
    mine, other = mine_ref[...].astype(F32), other_ref[...].astype(F32)
    chip = jnp.concatenate([(1.0 - core) * mine + core * other, (1.0 - core) * other + core * mine], 0)
    through = twin_ref[0:STATE, :].astype(F32) + factor_of(twin_ref, STATE) * chip
    arriving = ((1.0 - core) * chip + core * through).astype(BF16).astype(F32)
    carried = (1.0 - second + second * dec_ref[0:1, :]) * arriving + second * local_ref[...]
    crossed = contract(read_ref[...], carried.astype(BF16), 1, 0)
    fresh = 1.0 - start_ref[:, 0:1].astype(F32)
    reach = spread_wide(jnp.exp(sums_by_column(log_ref[...], tri)) * fresh, spread)
    gate = gate_ref[...].astype(F32)
    g = (direct_ref[...] + crossed * reach) * (gate / (1.0 + jnp.exp(-gate)))
    out_ref[...] = (g * gain_ref[...]).astype(BF16)
    squares = jnp.broadcast_to(jnp.sum(g * g, axis=1, keepdims=True), (block, 128))
    sq_ref[...] = jnp.transpose(squares)[0:8, :]


def assemble_kernel(where_ref, g_ref, *refs):
    own_ref, twin_ref, out_ref, w_ref = refs
    x_size, z_size, cores, rows, _ = w_ref.shape
    head, x_at, z_at, core = (where_ref[i] for i in range(4))

    def place(ref, base, x, k):
        way = jnp.where(k == 0, z_size - 1, 1)
        slots = [(z_at, k)]
        for turn in range(1, z_size // 2):
            z = (z_at + turn * way) % z_size
            slots += [(z, k), (z, 1 - k)]
        slots.append(((z_at + z_size // 2) % z_size, k))
        for slot, (z, block) in enumerate(slots):
            w_ref[x % x_size, z, block] = ref[base + slot]

    def one_x(turn, _):
        by = jnp.where(turn == 0, 0, jnp.where(turn == 1, x_size - 1, turn - 1))
        place(own_ref, turn * z_size, x_at + by, core)
        place(twin_ref, turn * z_size, x_at + by, 1 - core)

    lax.fori_loop(0, x_size, one_x, None)
    width = out_ref.shape[1]
    at = pl.multiple_of(((head + 2) % 4) * width, width)
    weights = w_ref[:, :, :, :, pl.ds(at, width)].reshape(g_ref.shape[1], width)
    out_ref[...] = contract(g_ref[...], weights, 1, 0).astype(BF16)


def product_kernel(head_ref, a_ref, w_ref, out_ref):
    weights = w_ref[...].reshape(a_ref.shape[1], w_ref.shape[-1])
    out_ref[0] = contract(a_ref[...], weights, 1, 0)


def down_kernel(where_ref, a_ref, w_ref, out_ref):
    block = a_ref.shape[1] // 4
    total = 0.0
    for x in range(4):
        weights = w_ref[:, (x - where_ref[1]) % 4].reshape(block, w_ref.shape[-1])
        total = total + contract(a_ref[:, x * block : (x + 1) * block], weights, 1, 0)
    out_ref[0] = total


def gained(ref, gain_ref, head, by):
    width = ref.shape[1]
    at = pl.multiple_of(((head + by) % 4) * width, width)
    return (ref[...].astype(F32) * gain_ref[:, pl.ds(at, width)]).astype(BF16)


def row_squares(ref):
    v = ref[...].astype(F32)
    return jnp.broadcast_to(jnp.sum(v * v, axis=1, keepdims=True), (ref.shape[0], 128))


def flat(ref):
    return ref[...].reshape(ref.shape[0] * ref.shape[1] * ref.shape[2], ref.shape[3])


def near_kernel(head_ref, own_ref, prev_ref, next_ref, gain_ref, w_ref, acc_ref, sq_ref, x_ref):
    step = pl.program_id(0)

    @pl.when(step == 0)
    def _():
        total = 0.0
        for slot, (ref, by) in enumerate([(own_ref, 0), (prev_ref, 3), (next_ref, 1)]):
            x_ref[slot] = gained(ref, gain_ref, head_ref[0], by)
            total = total + row_squares(ref)
        sq_ref[...] = total

    block = 256
    pairs = acc_ref.shape[1] // block // 2
    rows = w_ref.shape[0] * w_ref.shape[2]

    for n in range(2 * pairs):
        at, of = n * block, (n % 2 * pairs + n // 2) * block
        part = contract(x_ref[step], w_ref[:, 0, :, pl.ds(of, block)].reshape(rows, block), 1, 0)
        acc_ref[:, pl.ds(at, block)] = jnp.where(step == 0, part, acc_ref[:, pl.ds(at, block)] + part)


def act_kernel(
    head_ref, far_ref, gain_ref, w_gate_ref, w_up_ref, acc_ref, sq_ref, down_ref, act_ref, out_ref, x_ref, scale_ref, sum_ref
):
    step = pl.program_id(0)

    @pl.when(step == 0)
    def _():
        x_ref[...] = gained(far_ref, gain_ref, head_ref[0], 2)
        total = sq_ref[...] + row_squares(far_ref)
        scale_ref[...] = lax.rsqrt(total / (4 * far_ref.shape[1]) + EPS)
        sum_ref[...] = jnp.zeros_like(sum_ref)

    scale = scale_ref[:, 0:1]
    block = w_up_ref.shape[-1]
    gate = (acc_ref[:, :block] + contract(x_ref[...], flat(w_gate_ref), 1, 0)) * scale
    up = (acc_ref[:, block:] + contract(x_ref[...], flat(w_up_ref), 1, 0)) * scale
    act = (gate / (1.0 + jnp.exp(-gate)) * up).astype(BF16)
    act_ref[...] = act
    sum_ref[...] += contract(act, flat(down_ref), 1, 0)

    @pl.when(step == pl.num_programs(0) - 1)
    def _():
        out_ref[...] = sum_ref[...].astype(BF16)


def along_x(array, by, x_size, z_size):
    row = 2 * z_size
    return lax.ppermute(array, "ctx", [(i, (i + by * row) % (x_size * row)) for i in range(x_size * row)])


def moved(array, axis, x_size, z_size, far=1):
    pairs = []
    for x in range(x_size):
        for z in range(z_size):
            for core in range(2):
                by = far * (1 - 2 * core)
                to = {
                    "x": ((x + by) % x_size, z, core),
                    "z": (x, (z + by) % z_size, core),
                    "core": (x, z, 1 - core),
                }[axis]
                pairs.append(((x * z_size + z) * 2 + core, (to[0] * z_size + to[1]) * 2 + to[2]))
    return lax.ppermute(array, "ctx", pairs)


def sent(array, by):
    return lax.ppermute(array, "head", [(i, (i + by) % 4) for i in range(4)])


def scattered(far, parts, beside=None):
    half = far.shape[0] // 2
    first, second = sent(far[:half], 1), sent(far[half:], -1)
    if beside is not None:
        first, second, beside = lax.optimization_barrier((first, second, beside))
    one, three, own = parts()
    one = jnp.concatenate([one[:half] + first.astype(F32), one[half:]], 0).astype(BF16)
    three = jnp.concatenate([three[:half], three[half:] + second.astype(F32)], 0).astype(BF16)
    return own + sent(one, 1).astype(F32) + sent(three, -1).astype(F32), beside


def shards(
    mixer_input,
    gate_input,
    write_vecs,
    read_vecs,
    log_decay,
    doc_start,
    live_mask,
    skip_gain,
    norm_gain,
    residual,
    out_weight,
    mlp_gain,
    gate_weight,
    up_weight,
    down_weight,
):
    tokens, inner = mixer_input.shape
    heads = log_decay.shape[0]
    peers = lax.axis_size("ctx")
    width = residual.shape[1]
    model = out_weight.shape[1]
    units = gate_weight.shape[1]
    in_rows, ff_rows, out_rows = gate_weight.shape[0], down_weight.shape[0], out_weight.shape[0]
    x_size = 4
    z_size = peers // (2 * x_size)

    packed = jnp.concatenate([jnp.concatenate([gate_weight, up_weight], 1), down_weight], 0)

    in_hbm = lambda a: pltpu.with_memory_space_constraint(a, pltpu.HBM)
    mixer_input, gate_input, write_vecs, read_vecs, log_decay = map(
        in_hbm, (mixer_input, gate_input, write_vecs, read_vecs, log_decay)
    )
    starts = doc_start.reshape(1, tokens)
    live = live_mask.reshape(1, tokens)
    skip = jnp.repeat(skip_gain, HDIM).reshape(1, inner)
    gain = norm_gain.reshape(1, inner)
    at = lax.axis_index("ctx")
    where = jnp.stack([lax.axis_index("head"), at // (2 * z_size), at // 2 % z_size, at % 2])

    entire = lambda shape: pl.BlockSpec(shape, lambda i: (0,) * len(shape))
    state_in = (mixer_input, write_vecs, log_decay, starts, live)
    state_out = (((STATE + 16, inner), BF16), ((STATE, inner), F32), ((8, inner), F32))
    payload, local_0, dec_0 = pl.pallas_call(
        state_kernel,
        grid=(1,),
        out_shape=tuple(jax.ShapeDtypeStruct(*o) for o in state_out),
        in_specs=[entire(a.shape) for a in state_in],
        out_specs=tuple(entire(o[0]) for o in state_out),
        compiler_params=params(),
        name="state",
    )(*state_in)

    def passed(array, by):
        return lax.ppermute(array, "ctx", [(i, i + by) for i in range(peers - by)])

    def joined(kernel, name, *arrays):
        return pl.pallas_call(
            kernel,
            out_shape=jax.ShapeDtypeStruct((STATE // 2 + 16, inner), BF16),
            in_specs=[pl.BlockSpec(memory_space=pltpu.SMEM if a.ndim == 1 else pltpu.VMEM) for a in arrays],
            out_specs=vmem(),
            compiler_params=params(),
            name=name,
        )(*arrays)

    by_group = pl.BlockSpec((GROUP, inner), lambda g: (g, 0))
    vecs = pl.BlockSpec((GROUP, STATE), lambda g: (g, 0))
    logs = pl.BlockSpec((heads, GROUP), lambda g: (0, g))
    flags = pl.BlockSpec((1, GROUP), lambda g: (0, g))
    whole = lambda a: pl.BlockSpec(a.shape, lambda g: (0,) * a.ndim)
    some = heads // 2
    direct = pl.pallas_call(
        intra_kernel,
        grid=(tokens // GROUP, 2),
        out_shape=jax.ShapeDtypeStruct((tokens, inner), F32),
        in_specs=[
            pl.BlockSpec((GROUP, inner // 2), lambda g, k: (g, k)),
            pl.BlockSpec((GROUP, STATE), lambda g, k: (g, 0)),
            pl.BlockSpec((GROUP, STATE), lambda g, k: (g, 0)),
            pl.BlockSpec((some, GROUP), lambda g, k: (k, g)),
            pl.BlockSpec((1, GROUP), lambda g, k: (0, g)),
            pl.BlockSpec((1, inner // 2), lambda g, k: (0, k)),
        ],
        out_specs=pl.BlockSpec((GROUP, inner // 2), lambda g, k: (g, k)),
        compiler_params=params(),
        name="intra",
    )(mixer_input, write_vecs, read_vecs, log_decay, live, skip)

    step = lambda array, axis, far=1: moved(array, axis, x_size, z_size, far)
    tie = lambda *arrays: lax.optimization_barrier(arrays)
    block = out_weight[None]
    row = lambda array, by: along_x(array, by, x_size, z_size)
    other, packed = tie(step(block, "core"), packed)
    beyond = row(packed, -1), step(packed, "x", 2), row(packed, 1)
    piece = jnp.concatenate([block, other], 0)
    reach = z_size // 2
    first, *pieces = [step(piece, "z", far) for far in range(1, reach)] + [step(piece[:1], "z", reach)]
    twin = step(payload, "core")
    chips = joined(pair_kernel, "pair", where, payload, twin)
    got = passed(chips, 2)
    first, *pieces, next_x, over_x, last_x, got = tie(first, *pieces, *beyond, got)
    around_z = [list(range(x * 2 * z_size, (x + 1) * 2 * z_size)) for x in range(x_size)]
    weights = lax.all_gather(jnp.stack([packed, next_x, over_x, last_x]), "ctx", axis=0, axis_index_groups=around_z)
    chips, first = tie(joined(join_kernel, "join", chips, got), first)
    column_parts = [block, first, *pieces]
    column = pl.pallas_call(
        stack_kernel,
        out_shape=jax.ShapeDtypeStruct((z_size, out_rows, model), BF16),
        in_specs=[vmem()] * len(column_parts),
        out_specs=vmem(),
        compiler_params=params(),
        name="column",
    )(*column_parts)
    got, behind, ahead, direct = tie(passed(chips, 4), row(column, 1), row(column, -1), direct)
    chips, behind, ahead = tie(joined(join_kernel, "join", chips, got), behind, ahead)
    reached = passed(chips[: STATE // 2], 2)
    ends = row(behind[:reach], 1), row(ahead[reach:], -1)
    *ends, reached = tie(*ends, reached)
    own_out = jnp.concatenate([column, behind, ahead, *ends], 0)
    twin_out = step(own_out, "core")
    reached_twin = step(reached, "core")

    part = GROUP // 2
    by_part = pl.BlockSpec((part, inner), lambda i: (i, 0))
    gated, squares = pl.pallas_call(
        gate_kernel,
        grid=(tokens // part,),
        out_shape=(
            jax.ShapeDtypeStruct((tokens, inner), BF16),
            jax.ShapeDtypeStruct((8, tokens), F32),
        ),
        in_specs=[
            pl.BlockSpec(memory_space=pltpu.SMEM),
            by_part,
            whole(reached),
            whole(reached_twin),
            whole(twin),
            whole(local_0),
            whole(dec_0),
            pl.BlockSpec((part, STATE), lambda i: (i, 0)),
            pl.BlockSpec((heads, GROUP), lambda i: (0, i * part // GROUP)),
            pl.BlockSpec((1, GROUP), lambda i: (0, i * part // GROUP)),
            by_part,
            whole(gain),
        ],
        out_specs=(by_part, pl.BlockSpec((8, part), lambda i: (0, i))),
        compiler_params=params(),
        name="gating",
    )(where, direct, reached, reached_twin, twin, local_0, dec_0, read_vecs, log_decay, starts, gate_input, gain)
    mine = squares[0]
    pair = mine + sent(mine, 1)

    def call(kernel, grid, ins, outs, scratch, name, *args):
        return pl.pallas_call(
            kernel,
            grid_spec=pltpu.PrefetchScalarGridSpec(
                num_scalar_prefetch=1,
                grid=grid,
                in_specs=[spec for spec, _ in ins],
                out_specs=[spec for spec, _ in outs],
                scratch_shapes=scratch,
            ),
            out_shape=[shape for _, shape in outs],
            compiler_params=params(),
            name=name,
        )(*args, *[array for _, array in ins])

    def fixed(array):
        return pl.BlockSpec(array.shape, lambda j, h: (0,) * array.ndim), array

    def new(shape, dtype, block=None, index=None):
        index = index or (lambda j, h: (0,) * len(shape))
        return pl.BlockSpec(block or shape, index), jax.ShapeDtypeStruct(shape, dtype)

    share = (tokens, width)
    grid_of_rows = (x_size, z_size, 2, out_rows, model)
    far, rows_in_order = call(
        assemble_kernel,
        (1,),
        [fixed(a) for a in (gated, own_out, twin_out)],
        [new(share, BF16), new(grid_of_rows, BF16)],
        [],
        "assemble",
        where,
    )

    def others(kernel, array, spec, name):
        (parts,) = call(
            kernel,
            (3,),
            [fixed(array), spec],
            [new((3, *share), F32, (1, *share), lambda j, h: (j, 0, 0))],
            [],
            name,
            where,
        )
        return parts[0], parts[1], parts[2]

    part_of = lambda j, h: (h[0] + jnp.where(j == 2, 0, 2 * j + 1)) % 4
    by_column = pl.BlockSpec((*grid_of_rows[:4], width), lambda j, h: (0, 0, 0, 0, part_of(j, h)))
    far, pair = tie(far, pair)
    total = pair + sent(pair, 2)
    summed, total = scattered(far, lambda: others(product_kernel, gated, (by_column, rows_in_order), "project"), total)
    row_scale = lax.rsqrt(total / INNER + EPS)
    hidden = (residual.astype(F32) + summed * row_scale[:, None]).astype(BF16)

    half = tokens // 2
    mlp_gains = mlp_gain.reshape(1, model)
    blocks = 2 * z_size

    def rows_of(by, block, index):
        return pl.BlockSpec((blocks, 1, in_rows, block), lambda j, h: (0, (h[0] + by - h[1]) % 4, 0, index(j))), weights

    wide = (tokens, 2 * units)
    prev, following = sent(hidden, 1), sent(hidden, -1)
    prev, following, weights = tie(prev, following, weights)
    weights = in_hbm(weights)
    ends = sent(prev[:half], 1), sent(following[half:], -1)
    ff_block = 256
    ff_steps = units // ff_block
    acc, squares = call(
        near_kernel,
        (3,),
        [
            fixed(hidden),
            fixed(prev),
            fixed(following),
            fixed(mlp_gains),
            (
                pl.BlockSpec(
                    (blocks, 1, in_rows, 2 * units),
                    lambda j, h: (0, (h[0] + jnp.where(j == 1, 3, j // 2) - h[1]) % 4, 0, 0),
                ),
                weights,
            ),
        ],
        [new(wide, F32), new((tokens, 128), F32)],
        [pltpu.VMEM((3, *share), BF16)],
        "mlp_near",
        where,
    )
    down_spec = pl.BlockSpec(
        (blocks, 1, ff_rows, width), lambda j, h: (0, (j - h[1]) % 4, in_rows // ff_rows, (h[0] + 2) % 4)
    )
    act, far = call(
        act_kernel,
        (ff_steps,),
        [
            fixed(jnp.concatenate(ends, 0)),
            fixed(mlp_gains),
            rows_of(2, ff_block, lambda j: j),
            rows_of(2, ff_block, lambda j: ff_steps + j),
            (pl.BlockSpec((tokens, 2 * ff_block), lambda j, h: (0, j)), acc),
            fixed(squares),
            (down_spec, weights),
        ],
        [new((tokens, units), BF16, (tokens, ff_block), lambda j, h: (0, j)), new(share, BF16)],
        [pltpu.VMEM(share, BF16), pltpu.VMEM((tokens, 128), F32), pltpu.VMEM(share, F32)],
        "mlp_act",
        where,
    )
    by_column = pl.BlockSpec(
        (blocks, x_size, ff_rows, width),
        lambda j, h: (0, 0, in_rows // ff_rows, part_of(j, h)),
    )
    added, _ = scattered(far, lambda: others(down_kernel, act, (by_column, weights), "mlp_down"))
    return (live_mask.astype(F32)[:, None] * (hidden.astype(F32) + added)).astype(BF16)


def solution(mesh):
    return jax.shard_map(
        shards,
        mesh=mesh,
        in_specs=(
            P("ctx", "head"),
            P("ctx", "head"),
            P("ctx", None),
            P("ctx", None),
            P("head", "ctx"),
            P("ctx"),
            P("ctx"),
            P("head"),
            P("head"),
            P("ctx", "head"),
            P(("head", "ctx"), None),
            P(),
            P("ctx", "head"),
            P("ctx", "head"),
            P(("head", "ctx"), None),
        ),
        out_specs=P("ctx", "head"),
        check_vma=False,
    )
```
